32 devices in a mesh: dp: 8 (over y, x, core), tensor: 4 (over z).
Axes of the slice: x: 2, y: 2, z: 4, core: 2. Of those that a mesh axis runs over, the one named last changes fastest.
Arguments:
- hidden_in: float32 [6144, 2048], P('dp', 'tensor'), may hold values from -30 to 30
- gain: float32 [2048], replicated, may hold values from 0.5 to 1.5
- bias: float32 [2048], replicated, may hold values from -1 to 1
- w_qkv: bfloat16 [2048, 3, 2048], P(None, None, 'tensor'), may hold values from -0.125 to 0.125
- b_qkv: float32 [3, 2048], P(None, 'tensor'), may hold values from -1 to 1
- w_dense: bfloat16 [2048, 2048], P('tensor'), may hold values from -1.5 to 1.5
- b_dense: float32 [2048], P('tensor'), may hold values from -1 to 1
- w_fc1: bfloat16 [2048, 8192], P(None, 'tensor'), may hold values from -1 to 1
- b_fc1: float32 [8192], P('tensor'), may hold values from -1 to 1
- w_fc2: bfloat16 [8192, 2048], P('tensor'), may hold values from -0.0625 to 0.0625
- b_fc2: float32 [2048], P('tensor'), may hold values from -1 to 1
- cotangent: float32 [6144, 2048], P('dp', 'tensor'), may hold values from -6 to 6
- seq_lengths: int32 [3], replicated, may hold values from 1 to 32, 48 in all
- padding: int32 [3], replicated, may hold values from 0 to 127
- block_perm: int32 [48], replicated, may hold values from 0 to 47, each once
Outputs:
- output: float32 [6144, 2048], P('dp', 'tensor')
- grad_input: float32 [6144, 2048], P('dp', 'tensor')
- grad_gain: float32 [2048], P('tensor')
- grad_bias: float32 [2048], P('tensor')
- grad_w_qkv: float32 [2048, 3, 2048], P(None, None, 'tensor')
- grad_b_qkv: float32 [3, 2048], P(None, 'tensor')
- grad_w_dense: float32 [2048, 2048], P('tensor')
- grad_b_dense: float32 [2048], P('tensor')
- grad_w_fc1: float32 [2048, 8192], P(None, 'tensor')
- grad_b_fc1: float32 [8192], P('tensor')
- grad_w_fc2: float32 [8192, 2048], P('tensor')
- grad_b_fc2: float32 [2048], P('tensor')
- rms_output: float32 [], replicated
- rms_branch: float32 [], replicated
The draws below stay inside these ranges and needn't reach their ends.
Inputs may be any that keep to these rules, and one draw needn't show every extreme that they name: `seq_lengths`: the lengths sum to 48; the longest is exactly 32. `block_perm`: each block number appears once.
All inputs are finite; a program needn't handle non-finite values.
Results may differ from the reference program's by a relative error of at most 0.025.
Values may be sent and summed in bfloat16 or wider, within the bound.
No kernel may reach another device: no remote copies, remote signals or barrier semaphores. Data moves between devices by JAX's collectives and lax.ppermute only.
A program may use at most 256 MiB of HBM per device.

```python
import math
import jax
import jax.numpy as jnp
import numpy as np
from jax import lax

D = 2048
FF = 8192
HEADS = 32
HD = 64
ROT = 32
BLK = 128
MOSTB = 32
NBLK = 48
NSEQ = 3
TOKENS = 6144


def draw_hidden_in(key, part):
    first_key, second_key, third_key = jax.random.split(key, 3)
    row_index = jnp.arange(TOKENS, dtype=jnp.float32)[:, None]
    rising = 3.0 ** (row_index / TOKENS)
    rough_rows = jnp.exp(jax.random.uniform(first_key, (TOKENS, 1), minval=0.0, maxval=1.0986))
    rough_cols = jnp.exp(jax.random.uniform(second_key, (1, D), minval=0.0, maxval=0.6931))
    base = 0.4 * jax.random.truncated_normal(third_key, -4.0, 4.0, (TOKENS, D))
    return (base * rising * rough_rows * rough_cols).astype(jnp.float32)


def draw_w_fc1(key, part):
    own_key = jax.random.fold_in(key, 7)
    first_key, second_key = jax.random.split(own_key, 2)
    base = jax.random.truncated_normal(first_key, -4.0, 4.0, (D, FF))
    shared = jax.random.truncated_normal(second_key, -4.0, 4.0, (1, FF))
    return ((base + shared) * D ** (-0.5)).astype(jnp.float32).astype(jnp.bfloat16)


def level_of(key, shape, pieces, least, largest):
    def one(dim, blocks):
        steps = jax.random.uniform(jax.random.fold_in(jax.random.fold_in(key, 6), dim), (blocks,), jnp.float32, least / len(pieces), largest / len(pieces))
        return jnp.repeat(jnp.exp(steps), shape[dim] // blocks).reshape((-1,) + (1,) * (len(shape) - dim - 1))

    factor_of = one(*pieces[0])
    for cut in pieces[1:]:
        factor_of = factor_of * one(*cut)
    return factor_of


def split_up(amount, total, reach, slope):
    portions = [(1 << 20) // math.isqrt(rank ** slope) + 1 for rank in range(2, amount + 1)]
    spare, given = total - reach - (amount - 1), [1] * (amount - 1)
    while spare > 0:
        candidates = [i for i in range(amount - 1) if given[i] < reach]
        whole, left = sum([portions[i] for i in candidates]), spare
        for i in candidates:
            more = min(reach - given[i], max(1, left * portions[i] // whole), spare)
            given[i] = given[i] + more
            spare = spare - more
    return np.array([reach] + given)


def uneven(key, amount, total, most, skew):
    if amount == 2:
        one = jax.random.randint(key, (), max(1, total - most), min(most, total - 1) + 1)
        return jnp.stack([one, total - one])
    sizes = jnp.asarray(split_up(amount, total, most, skew), jnp.int32)
    twos = (amount - 1) // 2
    giver, taker = sizes[1:1 + 2 * twos:2], sizes[2:2 + 2 * twos:2]
    slack = jnp.minimum(giver - 1, most - taker)
    moved = jax.random.randint(jax.random.fold_in(key, 1), (twos,), 0, 1 << 20) % (slack + 1)
    sizes = sizes.at[1:1 + 2 * twos:2].set(giver - moved).at[2:2 + 2 * twos:2].set(taker + moved)
    return sizes[jax.random.permutation(jax.random.fold_in(key, 2), amount)]


def centred(key, dims, width, most, cuts=(), kind=jnp.bfloat16):
    loudness = level_of(key, dims, cuts, -0.22, 0.18) if cuts else 1.0
    values = jax.random.normal(key, dims, jnp.float32) * width * loudness
    return jnp.minimum(jnp.maximum(values, -most), most).astype(kind)


def setup_inputs(seed: int = 0) -> dict:
    seeds = jax.random.split(jax.random.key(seed), 16)
    hidden_in = draw_hidden_in(jax.random.fold_in(seeds[15], 71), 0)
    gain = jnp.clip(1.0 + 0.1 * jax.random.normal(seeds[1], (D,), jnp.float32), 0.5, 1.5)
    bias = centred(seeds[2], (D,), 0.2, 1.0, (), jnp.float32)
    w_qkv = centred(seeds[3], (D, 3, HEADS * HD), D ** -0.5, 0.125, ((2, 4),))
    b_qkv = centred(seeds[4], (3, HEADS * HD), 0.2, 1.0, ((1, 4),), jnp.float32)
    w_dense = centred(seeds[5], (HEADS * HD, D), (HEADS * HD // 128) ** -0.5, 1.5, ((0, 4),))
    b_dense = centred(seeds[6], (D,), 0.2, 1.0, ((0, 4),), jnp.float32)
    w_fc1 = draw_w_fc1(jax.random.fold_in(seeds[15], 71), 0)
    b_fc1 = centred(seeds[8], (FF,), 0.2, 1.0, ((0, 4),), jnp.float32)
    w_fc2 = centred(seeds[9], (FF, D), FF ** -0.5, 0.0625, ((0, 4),))
    b_fc2 = centred(seeds[10], (D,), 0.2, 1.0, ((0, 4),), jnp.float32)
    cotangent = centred(seeds[11], (TOKENS, D), 1.0, 6.0, ((0, 8), (1, 4)), jnp.float32)
    seq_lengths = uneven(seeds[12], NSEQ, NBLK, MOSTB, 2).astype(jnp.int32)
    padding = jax.random.randint(seeds[13], (NSEQ,), 0, BLK).astype(jnp.int32)
    block_perm = jax.random.permutation(seeds[14], NBLK).astype(jnp.int32)
    return {"hidden_in": hidden_in, "gain": gain, "bias": bias, "w_qkv": w_qkv, "b_qkv": b_qkv, "w_dense": w_dense, "b_dense": b_dense, "w_fc1": w_fc1, "b_fc1": b_fc1, "w_fc2": w_fc2, "b_fc2": b_fc2, "cotangent": cotangent, "seq_lengths": seq_lengths, "padding": padding, "block_perm": block_perm}


precise = lax.Precision.HIGHEST
epsilon = 1e-05

@jax.custom_vjp
def low(v):
    return lax.optimization_barrier(v.astype(jnp.bfloat16)).astype(jnp.float32)

@jax.custom_vjp
def low_back(v):
    return v

def low_keep(v):
    return (low(v), None)

def low_pass(kept, grad):
    return (grad,)

def back_keep(v):
    return (v, None)

def back_low(kept, grad):
    return (low(grad),)
low.defvjp(low_keep, low_pass)
low_back.defvjp(back_keep, back_low)

def token_table(seq_lengths, padding, initial):
    seq_count = seq_lengths.shape[0]
    seq_ends = jnp.cumsum(seq_lengths).astype(jnp.int32)
    seq_starts = seq_ends - seq_lengths
    seq_block = lax.optimization_barrier(jnp.sum((initial[:, None] >= seq_ends[None, :]).astype(jnp.int32), axis=1))
    members = (seq_block[:, None] == jnp.arange(seq_count, dtype=jnp.int32)[None, :]).astype(jnp.int32)
    first_block = lax.optimization_barrier(jnp.sum(members * seq_starts[None, :], axis=1))
    limits = lax.optimization_barrier(jnp.sum(members * (seq_lengths * BLK - padding)[None, :], axis=1))
    offsets = jnp.arange(BLK, dtype=jnp.int32)
    positions = (initial - first_block)[:, None] * BLK + offsets[None, :]
    seq_ids = jnp.broadcast_to(seq_block[:, None], positions.shape)
    is_valid = positions < limits[:, None]
    return (seq_ids.reshape(-1), positions.reshape(-1), is_valid.reshape(-1))

def rotary_tables(positions):
    frequency = 10000.0 ** (-jnp.arange(0, ROT, 2, dtype=jnp.float32) / ROT)
    angles = positions.astype(jnp.float32)[:, None] * frequency[None, :]
    return (jnp.cos(angles)[:, None, :], jnp.sin(angles)[:, None, :])

def rotate(heads_array, cosine_table, sine_table):
    half_rot = ROT // 2
    lower_half = heads_array[..., :half_rot]
    upper_half = heads_array[..., half_rot:ROT]
    return jnp.concatenate([lower_half * cosine_table - upper_half * sine_table, upper_half * cosine_table + lower_half * sine_table, heads_array[..., ROT:]], axis=-1)

def attention(queries, keys, values, seq_ids, positions):
    token_count = queries.shape[0]
    query_rows = min(512, token_count)
    window = MOSTB * BLK
    pad_keys = jnp.pad(keys, ((window, 0), (0, 0), (0, 0)))
    pad_values = jnp.pad(values, ((window, 0), (0, 0), (0, 0)))
    pad_seq = jnp.concatenate([jnp.full((window,), -1, jnp.int32), seq_ids.astype(jnp.int32)])
    pad_pos = jnp.concatenate([jnp.zeros((window,), jnp.int32), positions.astype(jnp.int32)])
    score_scale = HD ** (-0.5)

    def attend_rows(block_index):
        row_start = (block_index * query_rows).astype(jnp.int32)
        query_block = lax.dynamic_slice_in_dim(queries, row_start, query_rows, 0)
        query_seq = lax.dynamic_slice_in_dim(seq_ids, row_start, query_rows, 0)
        query_pos = lax.dynamic_slice_in_dim(positions, row_start, query_rows, 0)
        key_block = lax.dynamic_slice_in_dim(pad_keys, row_start, window + query_rows, 0)
        value_block = lax.dynamic_slice_in_dim(pad_values, row_start, window + query_rows, 0)
        key_seq = lax.dynamic_slice_in_dim(pad_seq, row_start, window + query_rows, 0)
        key_pos = lax.dynamic_slice_in_dim(pad_pos, row_start, window + query_rows, 0)
        scores = jnp.einsum('qhd,khd->hqk', query_block, key_block, precision=precise) * score_scale
        allowed = (key_seq[None, :] == query_seq[:, None]) & (key_pos[None, :] <= query_pos[:, None])
        scores = low_back(jnp.where(allowed[None], scores, -1e+30))
        probabilities = jax.nn.softmax(scores, axis=-1)
        return jnp.einsum('hqk,khd->qhd', low(probabilities), value_block, precision=precise)
    blocks = lax.map(jax.checkpoint(attend_rows), jnp.arange(token_count // query_rows, dtype=jnp.int32))
    return blocks.reshape(token_count, -1)

def reference(hidden_in, gain, bias, w_qkv, b_qkv, w_dense, b_dense, w_fc1, b_fc1, w_fc2, b_fc2, cotangent, seq_lengths, padding, block_perm):
    nblocks = block_perm.shape[0]
    token_count = nblocks * BLK
    inverse = jnp.zeros((nblocks,), jnp.int32).at[block_perm].set(jnp.arange(nblocks, dtype=jnp.int32))

    def undeal(matrix):
        return matrix.reshape(nblocks, BLK, -1)[inverse].reshape(token_count, -1)

    def redeal(matrix):
        return matrix.reshape(nblocks, BLK, -1)[block_perm].reshape(token_count, -1)
    seq_ids, positions, is_valid = token_table(seq_lengths, padding, jnp.arange(nblocks, dtype=jnp.int32))
    cosine_table, sine_table = rotary_tables(positions)

    def forward(residual, norm_gain, norm_bias, qkv_weight, qkv_bias, dense_weight, dense_bias, fc1_weight, fc1_bias, fc2_weight, fc2_bias):
        row_mean = lax.optimization_barrier(jnp.mean(residual, axis=-1, keepdims=True))
        centered = residual - row_mean
        variance = lax.optimization_barrier(jnp.mean(centered * centered, axis=-1, keepdims=True))
        normal_x = centered * lax.rsqrt(variance + epsilon)
        normed = low(normal_x * norm_gain + norm_bias)
        projections = low_back(jnp.einsum('td,dcf->tcf', normed, qkv_weight, precision=precise) + qkv_bias)
        shaped = projections.reshape(token_count, 3, HEADS, HD)
        queries = low(rotate(shaped[:, 0], cosine_table, sine_table))
        keys = low(rotate(shaped[:, 1], cosine_table, sine_table))
        values = low(shaped[:, 2])
        attended = low(low_back(attention(queries, keys, values, seq_ids, positions)))
        hidden_pre = low_back(jnp.dot(normed, fc1_weight, precision=precise) + fc1_bias)
        activated = low(jax.nn.gelu(hidden_pre, approximate=True))
        projected = low_back(jnp.dot(attended, dense_weight, precision=precise) + jnp.dot(activated, fc2_weight, precision=precise))
        branch = projected + dense_bias + fc2_bias
        return (residual + branch, branch)
    floats = (undeal(hidden_in), gain, bias, w_qkv.astype(jnp.float32), b_qkv, w_dense.astype(jnp.float32), b_dense, w_fc1.astype(jnp.float32), b_fc1, w_fc2.astype(jnp.float32), b_fc2)
    (output, branch), pullback = jax.vjp(forward, *floats)
    gradients = pullback((undeal(cotangent), jnp.zeros_like(branch)))
    valid_rows = is_valid.astype(jnp.float32)[:, None]
    valid_count = jnp.sum(is_valid.astype(jnp.float32)) * D
    rms_output = jnp.sqrt(jnp.sum(output * output * valid_rows) / valid_count)
    rms_branch = jnp.sqrt(jnp.sum(branch * branch * valid_rows) / valid_count)
    return (redeal(output), redeal(gradients[0]), gradients[1], gradients[2], gradients[3], gradients[4], gradients[5], gradients[6], gradients[7], gradients[8], gradients[9], gradients[10], rms_output, rms_branch)
```

```python
import functools

import jax
import jax.numpy as jnp
from jax import lax
from jax.experimental import pallas as pl
from jax.experimental.pallas import tpu as pltpu
from jax.sharding import PartitionSpec as P

HD = 64
ROT = 32
HALF = ROT // 2
BLK = 128
TILE = 512
LANES = 128

epsilon = 1e-05
masked_score = -1e30
far_score = 1e30
log2e = 1.4426950408889634
f32 = jnp.float32
bf16 = jnp.bfloat16


def token_table(seq_lengths, padding, initial):
    seq_count = seq_lengths.shape[0]
    seq_ends = jnp.cumsum(seq_lengths)
    seq_starts = seq_ends - seq_lengths
    seq_block = jnp.sum((initial[:, None] >= seq_ends[None, :]).astype(jnp.int32), axis=1)
    members = (seq_block[:, None] == jnp.arange(seq_count, dtype=jnp.int32)[None, :]).astype(
        jnp.int32
    )
    first_block = jnp.sum(members * seq_starts[None, :], axis=1)
    limits = jnp.sum(members * (seq_lengths * BLK - padding)[None, :], axis=1)
    offsets = jnp.arange(BLK, dtype=jnp.int32)
    positions = (initial - first_block)[:, None] * BLK + offsets[None, :]
    is_valid = positions < limits[:, None]
    return (positions.reshape(-1), is_valid.reshape(-1))


def rotary_tables(positions):
    frequency = 10000.0 ** (-jnp.arange(0, ROT, 2, dtype=f32) / ROT)
    angles = frequency[:, None] * positions.astype(f32)[None, :]
    return (jnp.cos(angles), jnp.sin(angles))


def gelu_tanh(gelu_input):
    return jax.nn.gelu(gelu_input, approximate=True)


def dot_f32(a, b):
    return lax.dot_general(a, b, (((1,), (0,)), ((), ())), preferred_element_type=f32)


def flip(block):
    return jnp.transpose(block.astype(f32)).astype(bf16)


def each_query_tile(seq_ref, rank_ref, seq_count, split, body):
    def one_seq(s, count):
        start = seq_ref[0, s] * BLK
        length = seq_ref[1, s] * BLK
        tiles = (length + TILE - 1) // TILE

        def one_tile(i, unused):
            if split == 1:
                body(start, length, i, tiles)
            else:

                @pl.when(lax.rem(count + i, split) == rank_ref[0])
                def _():
                    body(start, length, i, tiles)

            return unused

        lax.fori_loop(0, tiles, one_tile, 0)
        return count + tiles

    lax.fori_loop(0, seq_count, one_seq, 0)


def forward_kernel(seq_count, slots, subs, split, place_ref, seq_ref, rank_ref, *refs):
    parts, outs, lse_ref, seq_out_ref, q_t, keys, v_t = refs
    tokens = slots * subs * BLK
    tail = q_t.shape[1] - tokens
    q_t[:, pl.ds(tokens, tail)] = jnp.zeros((HD, tail), bf16)
    v_t[:, pl.ds(tokens, tail)] = jnp.zeros((HD, tail), bf16)
    keys[pl.ds(tokens, tail), :] = jnp.zeros((tail, HD), bf16)
    if split > 1:
        lse_ref[...] = jnp.zeros(lse_ref.shape, f32)
        seq_out_ref[...] = jnp.zeros(seq_out_ref.shape, bf16)
    for s in range(slots):
        for b in range(subs):
            where = pl.multiple_of(place_ref[s * subs + b] * BLK, BLK)
            cols = slice(b * BLK, (b + 1) * BLK)
            q_t[:, pl.ds(where, BLK)] = parts[s, 0:HD, cols]
            keys[pl.ds(where, BLK), :] = flip(parts[s, HD : 2 * HD, cols])
            v_t[:, pl.ds(where, BLK)] = parts[s, 2 * HD :, cols]
    scale = HD ** (-0.5) * log2e
    row = lax.broadcasted_iota(jnp.int32, (TILE, TILE), 0)
    col = lax.broadcasted_iota(jnp.int32, (TILE, TILE), 1)

    def tile(start, length, i, tiles):
        q_at = pl.multiple_of(start + i * TILE, BLK)
        q_tile = q_t[:, pl.ds(q_at, TILE)]

        def step(j, carried, diagonal):
            run_max, run_sum, acc = carried
            k_at = pl.multiple_of(start + j * TILE, BLK)
            scores = dot_f32(keys[pl.ds(k_at, TILE), :], q_tile) * scale
            if diagonal:
                scores = jnp.where(row <= col, scores, masked_score)
            new_max = jnp.maximum(run_max, jnp.max(scores, axis=0, keepdims=True))
            factor = jnp.exp2(run_max - new_max)
            weights = jnp.exp2(scores - new_max)
            run_sum = run_sum * factor + jnp.sum(weights, axis=0, keepdims=True)
            acc = acc * factor + dot_f32(v_t[:, pl.ds(k_at, TILE)], weights.astype(bf16))
            return new_max, run_sum, acc

        carried = (
            jnp.full((1, TILE), masked_score, f32),
            jnp.zeros((1, TILE), f32),
            jnp.zeros((HD, TILE), f32),
        )
        carried = lax.fori_loop(0, i, lambda j, c: step(j, c, False), carried)
        run_max, run_sum, acc = step(i, carried, True)
        lse_ref[:, pl.ds(q_at, TILE)] = jnp.broadcast_to(run_max + jnp.log2(run_sum), (8, TILE))
        seq_out_ref[:, pl.ds(q_at, TILE)] = (acc / run_sum).astype(bf16)

    each_query_tile(seq_ref, rank_ref, seq_count, split, tile)
    for s in range(slots):
        for b in range(subs):
            where = pl.multiple_of(place_ref[s * subs + b] * BLK, BLK)
            outs[s, :, b * BLK : (b + 1) * BLK] = seq_out_ref[:, pl.ds(where, BLK)]


def backward_kernel(seq_count, slots, subs, split, place_ref, seq_ref, rank_ref, *refs):
    parts, grads, lse_ref, seq_out_ref, cos_ref, sin_ref, outs = refs[:7]
    k_t, q_up, g_down, kv, q_left, g_right, row_dot, dq_t, dkv = refs[7:]
    tokens = slots * subs * BLK
    tail = k_t.shape[1] - tokens
    q_up[HD:, :] = jnp.zeros((HD, tokens + tail), bf16)
    g_down[:HD, :] = jnp.zeros((HD, tokens + tail), bf16)
    k_t[:, pl.ds(tokens, tail)] = jnp.zeros((HD, tail), bf16)
    q_up[:HD, pl.ds(tokens, tail)] = jnp.zeros((HD, tail), bf16)
    g_down[HD:, pl.ds(tokens, tail)] = jnp.zeros((HD, tail), bf16)
    row_dot[:, pl.ds(tokens, tail)] = jnp.zeros((8, tail), f32)
    for wide in (kv, q_left, g_right):
        wide[pl.ds(tokens, tail), :] = jnp.zeros((tail, 2 * HD), bf16)
    dq_t[...] = jnp.zeros(dq_t.shape, f32)
    dkv[...] = jnp.zeros(dkv.shape, f32)
    left = lax.broadcasted_iota(jnp.int32, (BLK, 2 * HD), 1) < HD
    for s in range(slots):
        for b in range(subs):
            where = pl.multiple_of(place_ref[s * subs + b] * BLK, BLK)
            cols = slice(b * BLK, (b + 1) * BLK)
            at = pl.ds(where, BLK)
            q_blk = parts[s, 0:HD, cols]
            g_blk = grads[s, :, cols]
            q_up[:HD, at] = q_blk
            g_down[HD:, at] = g_blk
            k_t[:, at] = parts[s, HD : 2 * HD, cols]
            kv[at, :] = flip(parts[s, HD:, cols])
            both = jnp.transpose(jnp.concatenate([q_blk.astype(f32), g_blk.astype(f32)], axis=0))
            q_left[at, :] = jnp.where(left, both, 0.0).astype(bf16)
            g_right[at, :] = jnp.where(left, 0.0, both).astype(bf16)
            dots = jnp.sum(
                g_blk.astype(f32) * seq_out_ref[:, at].astype(f32), axis=0, keepdims=True
            )
            row_dot[:, at] = jnp.broadcast_to(dots, (8, BLK))
    scale = HD ** (-0.5)
    row = lax.broadcasted_iota(jnp.int32, (TILE, TILE), 0)
    col = lax.broadcasted_iota(jnp.int32, (TILE, TILE), 1)
    lane = lax.broadcasted_iota(jnp.int32, (1, TILE), 1)

    def pair(start, length, i, j, diagonal):
        q_at = pl.ds(pl.multiple_of(start + i * TILE, BLK), TILE)
        k_at = pl.ds(pl.multiple_of(start + j * TILE, BLK), TILE)
        lse = jnp.where(i * TILE + lane < length, lse_ref[0:1, q_at], far_score)
        kv_tile = kv[k_at, :]
        scores = dot_f32(kv_tile, q_up[:, q_at]) * (scale * log2e)
        if diagonal:
            scores = jnp.where(row <= col, scores, masked_score)
        probs = jnp.exp2(scores - lse)
        grad_probs = dot_f32(kv_tile, g_down[:, q_at])
        grad_scores = (probs * (grad_probs - row_dot[0:1, q_at])).astype(bf16)
        probs = probs.astype(bf16)
        dkv[k_at, :] += dot_f32(grad_scores, q_left[q_at, :]) + dot_f32(probs, g_right[q_at, :])
        return dot_f32(k_t[:, k_at], grad_scores)

    def tile(start, length, i, tiles):
        total = pair(start, length, i, i, True)
        total = lax.fori_loop(
            0, i, lambda j, c: c + pair(start, length, i, j, False), total
        )
        dq_t[:, pl.ds(pl.multiple_of(start + i * TILE, BLK), TILE)] = total

    each_query_tile(seq_ref, rank_ref, seq_count, split, tile)

    def unrotate(head_block, cosine, sine):
        lower = head_block[:HALF]
        upper = head_block[HALF:ROT]
        return jnp.concatenate(
            [
                lower * cosine + upper * sine,
                upper * cosine - lower * sine,
                head_block[ROT:],
            ],
            axis=0,
        )

    for s in range(slots):
        for b in range(subs):
            where = pl.multiple_of(place_ref[s * subs + b] * BLK, BLK)
            at = pl.ds(where, BLK)
            first = pl.multiple_of(place_ref[slots * subs + s * subs + b] * BLK, BLK)
            cosine = cos_ref[:, pl.ds(first, BLK)]
            sine = sin_ref[:, pl.ds(first, BLK)]
            cols = slice(b * BLK, (b + 1) * BLK)
            outs[s, 0:HD, cols] = unrotate(dq_t[:, at] * scale, cosine, sine).astype(bf16)
            pair_t = jnp.transpose(dkv[at, :])
            outs[s, HD : 2 * HD, cols] = unrotate(pair_t[:HD] * scale, cosine, sine).astype(bf16)
            outs[s, 2 * HD :, cols] = pair_t[HD:].astype(bf16)


def whole_vmem(count):
    return [pl.BlockSpec(memory_space=pltpu.VMEM)] * count


def attention_forward(place, seq, rank, parts, split):
    slots, unused, local_tokens = parts.shape
    tokens = slots * local_tokens
    padded = tokens + TILE
    pairs = tokens * tokens // 2
    return pl.pallas_call(
        functools.partial(forward_kernel, seq.shape[1], slots, local_tokens // BLK, split),
        name="attention_forward",
        out_shape=[
            jax.ShapeDtypeStruct((slots, HD, local_tokens), bf16),
            jax.ShapeDtypeStruct((8, padded), f32),
            jax.ShapeDtypeStruct((HD, padded), bf16),
        ],
        grid_spec=pltpu.PrefetchScalarGridSpec(
            num_scalar_prefetch=3,
            grid=(),
            in_specs=whole_vmem(1),
            out_specs=whole_vmem(3),
            scratch_shapes=[
                pltpu.VMEM((HD, padded), bf16),
                pltpu.VMEM((padded, HD), bf16),
                pltpu.VMEM((HD, padded), bf16),
            ],
        ),
        compiler_params=pltpu.CompilerParams(vmem_limit_bytes=60 * 2**20),
        cost_estimate=pl.CostEstimate(
            flops=16 * pairs * HD, bytes_accessed=tokens * HD * 12, transcendentals=pairs
        ),
    )(place, seq, rank, parts)


def attention_backward(place, seq, rank, parts, grads, lse, seq_out, cosine, sine, split):
    slots, unused, local_tokens = parts.shape
    tokens = slots * local_tokens
    padded = tokens + TILE
    pairs = tokens * tokens // 2
    return pl.pallas_call(
        functools.partial(backward_kernel, seq.shape[1], slots, local_tokens // BLK, split),
        name="attention_backward",
        out_shape=jax.ShapeDtypeStruct((slots, 3 * HD, local_tokens), bf16),
        grid_spec=pltpu.PrefetchScalarGridSpec(
            num_scalar_prefetch=3,
            grid=(),
            in_specs=whole_vmem(6),
            out_specs=whole_vmem(1)[0],
            scratch_shapes=[
                pltpu.VMEM((HD, padded), bf16),
                pltpu.VMEM((2 * HD, padded), bf16),
                pltpu.VMEM((2 * HD, padded), bf16),
                pltpu.VMEM((padded, 2 * HD), bf16),
                pltpu.VMEM((padded, 2 * HD), bf16),
                pltpu.VMEM((padded, 2 * HD), bf16),
                pltpu.VMEM((8, padded), f32),
                pltpu.VMEM((HD, padded), f32),
                pltpu.VMEM((padded, 2 * HD), f32),
            ],
        ),
        compiler_params=pltpu.CompilerParams(vmem_limit_bytes=62 * 2**20),
        cost_estimate=pl.CostEstimate(
            flops=40 * pairs * HD, bytes_accessed=tokens * HD * 24, transcendentals=pairs
        ),
    )(place, seq, rank, parts, grads, lse, seq_out, cosine, sine)


def swap(value, axis, size, offset):
    return lax.ppermute(value, axis, [(i, i ^ offset) for i in range(size)])


def axis_bits(size):
    return [1 << k for k in range(size.bit_length() - 1)]


def all_sum(value, axis, size):
    for bit in axis_bits(size):
        value = value + swap(value, axis, size, bit)
    return value


def slot_order(bits):
    if not bits:
        return [0]
    rest = slot_order(bits[1:])
    return [s | bits[0] for s in rest] + rest


def product_kernel(lhs_dim, rhs_dim, cuts, with_add, order_ref, lhs_ref, rhs_ref, *refs):
    step = pl.program_id(0)
    piece = lax.dot_general(
        lhs_ref[...], rhs_ref[...], (((lhs_dim,), (rhs_dim,)), ((), ())), preferred_element_type=f32
    )
    if with_add:
        piece = piece + refs[0][...].astype(f32)
    piece = piece.astype(bf16)
    outs = refs[1:] if with_add else refs
    for out, first, count in zip(outs, cuts, cuts[1:] + [None]):
        if len(outs) == 1:
            out[...] = piece
        else:
            inside = step >= first if count is None else (step >= first) & (step < count)

            @pl.when(inside)
            def _(out=out):
                out[...] = piece


def piece_products(owners, lhs, rhs, lhs_dim, rhs_dim, columns, half, added, cuts):
    steps = owners[0].shape[0]
    size = owners[1]
    rows = lhs.shape[1 - lhs_dim] // size
    tokens = lhs.shape[lhs_dim]
    table = owners[0].astype(jnp.int32)
    if added is not None:
        table = jnp.concatenate([table, jnp.array(added[1], jnp.int32)])
    lhs_block = (tokens, rows) if lhs_dim == 0 else (rows, tokens)
    rhs_block = (tokens, columns) if rhs_dim == 0 else (columns, tokens)
    in_specs = [
        pl.BlockSpec(lhs_block, (lambda i, t: (0, t[i])) if lhs_dim == 0 else (lambda i, t: (t[i], 0))),
        pl.BlockSpec(rhs_block, (lambda i, t: (0, half)) if rhs_dim == 0 else (lambda i, t: (half, 0))),
    ]
    operands = [lhs, rhs]
    if added is not None:
        in_specs.append(pl.BlockSpec((rows, columns), lambda i, t: (t[steps + i], half)))
        operands.append(added[0])
    ends = cuts[1:] + [steps]
    out_specs = [
        pl.BlockSpec(
            (rows, columns),
            lambda i, t, first=first, last=end - 1: (jnp.clip(i, first, last) - first, 0),
        )
        for first, end in zip(cuts, ends)
    ]
    return pl.pallas_call(
        functools.partial(product_kernel, lhs_dim, rhs_dim, cuts, added is not None),
        name="piece_products",
        out_shape=[
            jax.ShapeDtypeStruct((rows * (end - first), columns), bf16)
            for first, end in zip(cuts, ends)
        ],
        grid_spec=pltpu.PrefetchScalarGridSpec(
            num_scalar_prefetch=1, grid=(steps,), in_specs=in_specs, out_specs=out_specs
        ),
        compiler_params=pltpu.CompilerParams(vmem_limit_bytes=48 * 2**20),
        cost_estimate=pl.CostEstimate(
            flops=2 * steps * rows * columns * tokens,
            bytes_accessed=2 * (steps * rows * (tokens + columns * 2) + columns * tokens),
            transcendentals=0,
        ),
    )(table, *operands)


def halves_orders(size):
    upper = axis_bits(size)[1:]
    return [(upper, slot_order(upper)), (upper[::-1], slot_order(upper[::-1]))]


def piece_sums(index, size, lhs, rhs, lhs_dim, rhs_dim):
    orders = halves_orders(size)
    columns = rhs.shape[1 - rhs_dim]
    if lhs_dim == 0 and (lhs.shape[1] // size) % LANES:
        lhs, lhs_dim = jnp.transpose(lhs), 1
    first_order = orders[0][1]
    far = index ^ jnp.array([s | 1 for s in first_order], jnp.int32)
    sent = piece_products((far, size), lhs, rhs, lhs_dim, rhs_dim, columns, 0, None, [0])[0]
    got = swap(sent, "dp", size, 1)
    pieces = []
    for half, (bits, order) in enumerate(orders):
        near = index ^ jnp.array(order, jnp.int32)
        rows_at = [first_order.index(s) for s in order]
        send, keep = piece_products(
            (near, size), lhs, rhs, lhs_dim, rhs_dim, columns // 2, half, (got, rows_at),
            [0, size // 4],
        )
        for bit in bits:
            got_piece = swap(send, "dp", size, bit)
            cut = keep.shape[0] // 2
            if bit == bits[-1]:
                keep = (keep.astype(f32) + got_piece.astype(f32)).astype(bf16)
            else:
                send = (keep[:cut].astype(f32) + got_piece[:cut].astype(f32)).astype(bf16)
                keep = (keep[cut:].astype(f32) + got_piece[cut:].astype(f32)).astype(bf16)
        pieces.append(keep)
    return pieces


def spread_kernel(quarter, parts, table_ref, *refs):
    ins, out = refs[:-1], refs[-1]
    step = pl.program_id(0)
    for j, piece in enumerate(ins):

        @pl.when(step // quarter == j)
        def _(piece=piece):
            if parts == 1:
                out[...] = piece[...].astype(f32)
            else:
                wide = piece.shape[1] // parts
                for c in range(parts):
                    out[:, c, :] = piece[:, c * wide : (c + 1) * wide].astype(f32)


def spread(index, size, pieces, parts):
    arrays, slots = [], []
    for (bits, unused), piece in zip(halves_orders(size), pieces):
        have, have_slots = piece, [0]
        for bit in bits[:0:-1]:
            have = jnp.concatenate([have, swap(have, "dp", size, bit)], axis=0)
            have_slots = have_slots + [s | bit for s in have_slots]
        other = swap(have, "dp", size, bits[0])
        other_slots = [s | bits[0] for s in have_slots]
        arrays += [have, other, swap(have, "dp", size, 1), swap(other, "dp", size, 1)]
        slots += have_slots + other_slots
        slots += [s | 1 for s in have_slots] + [s | 1 for s in other_slots]
    table = index ^ jnp.array(slots, jnp.int32)
    quarter = size // 4
    rows, columns = pieces[0].shape
    in_specs = [
        pl.BlockSpec(
            (rows, columns),
            lambda i, t, at=j * quarter: (jnp.clip(i - at, 0, quarter - 1), 0),
        )
        for j in range(8)
    ]
    if parts == 1:
        out_shape = (rows * size, 2 * columns)
        out_spec = pl.BlockSpec((rows, columns), lambda i, t: (t[i], i // size))
    else:
        out_shape = (rows * size, parts, 2 * columns // parts)
        out_spec = pl.BlockSpec(
            (rows, parts, columns // parts), lambda i, t: (t[i], 0, i // size)
        )
    return pl.pallas_call(
        functools.partial(spread_kernel, quarter, parts),
        name="spread",
        out_shape=jax.ShapeDtypeStruct(out_shape, f32),
        grid_spec=pltpu.PrefetchScalarGridSpec(
            num_scalar_prefetch=1, grid=(2 * size,), in_specs=in_specs, out_specs=out_spec
        ),
        compiler_params=pltpu.CompilerParams(vmem_limit_bytes=48 * 2**20),
        cost_estimate=pl.CostEstimate(
            flops=0, bytes_accessed=rows * columns * size * 12, transcendentals=0
        ),
    )(table, *arrays)


def local(
    dp_size,
    hidden_in,
    gain,
    bias,
    w_qkv,
    b_qkv,
    w_dense,
    b_dense,
    w_fc1,
    b_fc1,
    w_fc2,
    b_fc2,
    cotangent,
    seq_lengths,
    padding,
    block_perm,
):
    tok_local, dim_local = hidden_in.shape
    model_width = gain.shape[0]
    heads = w_qkv.shape[2] // HD
    split = dp_size // heads
    subs = tok_local // BLK
    nblk = block_perm.shape[0]
    data_index = lax.axis_index("dp")
    tensor_index = lax.axis_index("tensor")
    pos_all, valid_all = token_table(seq_lengths, padding, block_perm)
    my_pos = lax.dynamic_slice_in_dim(pos_all, data_index * tok_local, tok_local)
    my_valid = lax.dynamic_slice_in_dim(valid_all, data_index * tok_local, tok_local)
    cosine, sine = rotary_tables(my_pos)
    cosine_all, sine_all = rotary_tables(jnp.arange(nblk * BLK, dtype=jnp.int32))
    place = jnp.concatenate([block_perm, pos_all[::BLK] // BLK])
    seq = jnp.stack([jnp.cumsum(seq_lengths) - seq_lengths, seq_lengths])
    rank = (data_index // heads).reshape(1).astype(jnp.int32)

    def to_heads(stacked):
        stacked = jnp.concatenate([stacked] * split) if split > 1 else stacked
        return lax.all_to_all(stacked, "dp", 0, 0, tiled=True)

    def to_tokens(stacked):
        got = lax.all_to_all(stacked, "dp", 0, 0, tiled=True)
        if split > 1:
            got = got.reshape(split, heads, *got.shape[1:]).astype(f32)
            got = jnp.sum(got, axis=0).astype(bf16)
        return got

    full_in = lax.all_gather(hidden_in.astype(bf16), "tensor", axis=1, tiled=True).astype(f32)
    grad_proj = lax.all_gather(cotangent.astype(bf16), "tensor", axis=1, tiled=True)
    row_mean = jnp.mean(full_in, axis=-1, keepdims=True)
    centered = full_in - row_mean
    inv_std = lax.rsqrt(jnp.mean(centered * centered, axis=-1, keepdims=True) + epsilon)
    normal_x = centered * inv_std
    normed = (normal_x * gain + bias).astype(bf16)
    projections = (
        jnp.einsum("td,dcf->cft", normed, w_qkv, preferred_element_type=f32) + b_qkv[:, :, None]
    ).reshape(3, heads, HD, tok_local)
    turned = projections[:2, :, :ROT].reshape(2, heads, 2, HALF, tok_local)
    lower, upper = turned[:, :, 0], turned[:, :, 1]
    rotated = jnp.concatenate(
        [
            lower * cosine - upper * sine,
            upper * cosine + lower * sine,
            projections[:2, :, ROT:],
        ],
        axis=2,
    )
    packed = jnp.concatenate([rotated[0], rotated[1], projections[2]], axis=1).astype(bf16)
    parts = to_heads(packed)
    out_stack, lse, seq_out = attention_forward(place, seq, rank, parts, split)
    attended = to_tokens(out_stack).reshape(heads * HD, tok_local)

    hidden_pre = jnp.dot(normed, w_fc1, preferred_element_type=f32) + b_fc1
    activated = gelu_tanh(hidden_pre).astype(bf16)
    partial_value = jnp.einsum(
        "et,ed->td", attended, w_dense, preferred_element_type=f32
    ) + jnp.dot(activated, w_fc2, preferred_element_type=f32)
    projected = lax.psum_scatter(
        partial_value.astype(bf16), "tensor", scatter_dimension=1, tiled=True
    ).astype(f32)
    branch = projected + b_dense + b_fc2
    output = hidden_in + branch
    valid_rows = my_valid.astype(f32)[:, None]
    sum_output = jnp.sum(output * output * valid_rows)
    sum_branch = jnp.sum(branch * branch * valid_rows)
    valid_count = jnp.sum(valid_all.astype(f32)) * model_width

    grad_attended = jnp.einsum(
        "ed,td->et", w_dense, grad_proj, preferred_element_type=f32
    ).astype(bf16)
    grad_stack = to_heads(grad_attended.reshape(heads, HD, tok_local))
    grad_act = jnp.einsum("td,fd->tf", grad_proj, w_fc2, preferred_element_type=f32)
    unused_value, gelu_back = jax.vjp(gelu_tanh, hidden_pre)
    grad_hidden = gelu_back(grad_act)[0].astype(bf16)
    grad_b_fc1 = jnp.sum(grad_hidden.astype(f32), axis=0)
    grad_normed = jnp.einsum("tf,df->td", grad_hidden, w_fc1, preferred_element_type=f32)

    def weight_sum(lhs, rhs, lhs_dim, rhs_dim, parts_out):
        pieces = piece_sums(data_index, dp_size, lhs, rhs, lhs_dim, rhs_dim)
        return spread(data_index, dp_size, pieces, parts_out)

    grad_w_fc2 = weight_sum(activated, grad_proj, 0, 0, 1)
    grad_w_fc1 = weight_sum(normed, grad_hidden, 0, 0, 1)
    grad_w_dense = weight_sum(attended, grad_proj, 1, 0, 1)

    early = jnp.concatenate(
        [jnp.sum(cotangent, axis=0), grad_b_fc1, sum_output[None], sum_branch[None]]
    )
    early = all_sum(early, "dp", dp_size)
    totals = all_sum(early[-2:], "tensor", model_width // dim_local)

    grad_pieces = attention_backward(
        place, seq, rank, parts, grad_stack, lse, seq_out, cosine_all, sine_all, split
    )
    grad_qkv = to_tokens(grad_pieces).reshape(heads, 3, HD, tok_local)
    grad_b_qkv = jnp.transpose(jnp.sum(grad_qkv.astype(f32), axis=3), (1, 0, 2))
    by_half = jnp.transpose(
        grad_qkv.reshape(2, heads // 2, 3, HD, tok_local), (0, 2, 1, 3, 4)
    ).reshape(3 * heads * HD, tok_local)
    grad_w_qkv = weight_sum(normed, by_half, 0, 1, 3)
    grad_normed = grad_normed + jnp.einsum(
        "hcet,dche->td",
        grad_qkv,
        w_qkv.reshape(model_width, 3, heads, HD),
        preferred_element_type=f32,
    )
    grad_local = lax.psum_scatter(
        grad_normed.astype(bf16), "tensor", scatter_dimension=1, tiled=True
    ).astype(f32)
    scaled = grad_normed * gain
    mean_sums = jnp.stack([jnp.sum(scaled, axis=1), jnp.sum(scaled * normal_x, axis=1)])
    mean_sums = all_sum(mean_sums, "tensor", model_width // dim_local) / model_width
    mean_one, mean_two = mean_sums[0][:, None], mean_sums[1][:, None]
    gain_local = lax.dynamic_slice_in_dim(gain, tensor_index * dim_local, dim_local)
    normal_local = lax.dynamic_slice_in_dim(normal_x, tensor_index * dim_local, dim_local, 1)
    grad_input = cotangent + inv_std * (
        grad_local * gain_local - mean_one - normal_local * mean_two
    )
    late = jnp.concatenate(
        [
            jnp.sum(grad_local * normal_local, axis=0),
            jnp.sum(grad_local, axis=0),
            grad_b_qkv.reshape(-1),
        ]
    )
    late = all_sum(late, "dp", dp_size)
    rms = jnp.sqrt(totals / valid_count)
    bias_grad = early[:dim_local]
    return (
        output,
        grad_input,
        late[:dim_local],
        late[dim_local : 2 * dim_local],
        grad_w_qkv,
        late[2 * dim_local :].reshape(3, heads * HD),
        grad_w_dense,
        bias_grad,
        grad_w_fc1,
        early[dim_local:-2],
        grad_w_fc2,
        bias_grad,
        rms[0],
        rms[1],
    )


def solution(mesh):
    return jax.shard_map(
        functools.partial(local, mesh.shape["dp"]),
        mesh=mesh,
        in_specs=(
            P("dp", "tensor"),
            P(),
            P(),
            P(None, None, "tensor"),
            P(None, "tensor"),
            P("tensor", None),
            P("tensor"),
            P(None, "tensor"),
            P("tensor"),
            P("tensor", None),
            P("tensor"),
            P("dp", "tensor"),
            P(),
            P(),
            P(),
        ),
        out_specs=(
            P("dp", "tensor"),
            P("dp", "tensor"),
            P("tensor"),
            P("tensor"),
            P(None, None, "tensor"),
            P(None, "tensor"),
            P("tensor", None),
            P("tensor"),
            P(None, "tensor"),
            P("tensor"),
            P("tensor", None),
            P("tensor"),
            P(),
            P(),
        ),
        check_vma=False,
    )
```

```python
import functools

import jax
import jax.numpy as jnp
from jax import lax
from jax.experimental import pallas as pl
from jax.experimental.layout import Layout, with_layout_constraint
from jax.experimental.pallas import tpu as pltpu
from jax.sharding import PartitionSpec as P

HD = 64
ROT = 32
HALF = ROT // 2
BLK = 128
TILE = 512

epsilon = 1e-05
masked_score = -1e30
far_score = 1e30
log2e = 1.4426950408889634
f32 = jnp.float32
bf16 = jnp.bfloat16


def row_major(value):
    return with_layout_constraint(value, Layout(tuple(range(value.ndim))))


def token_table(seq_lengths, padding, initial):
    seq_count = seq_lengths.shape[0]
    seq_ends = jnp.cumsum(seq_lengths)
    seq_starts = seq_ends - seq_lengths
    seq_block = jnp.sum((initial[:, None] >= seq_ends[None, :]).astype(jnp.int32), axis=1)
    members = (seq_block[:, None] == jnp.arange(seq_count, dtype=jnp.int32)[None, :]).astype(
        jnp.int32
    )
    first_block = jnp.sum(members * seq_starts[None, :], axis=1)
    limits = jnp.sum(members * (seq_lengths * BLK - padding)[None, :], axis=1)
    offsets = jnp.arange(BLK, dtype=jnp.int32)
    positions = (initial - first_block)[:, None] * BLK + offsets[None, :]
    is_valid = positions < limits[:, None]
    return (positions.reshape(-1), is_valid.reshape(-1))


def rotary_tables(positions):
    frequency = 10000.0 ** (-jnp.arange(0, ROT, 2, dtype=f32) / ROT)
    angles = frequency[:, None] * positions.astype(f32)[None, :]
    return (jnp.cos(angles), jnp.sin(angles))


def gelu_tanh(gelu_input):
    return jax.nn.gelu(gelu_input, approximate=True)


def dot_f32(a, b):
    return lax.dot_general(a, b, (((1,), (0,)), ((), ())), preferred_element_type=f32)


def flip(block):
    return jnp.transpose(block.astype(f32)).astype(bf16)


def each_query_tile(seq_ref, rank_ref, seq_count, split, body):
    def one_seq(s, count):
        start = seq_ref[0, s] * BLK
        length = seq_ref[1, s] * BLK
        tiles = (length + TILE - 1) // TILE

        def one_tile(i, unused):
            if split == 1:
                body(start, length, i, tiles)
            else:

                @pl.when(lax.rem(count + i, split) == rank_ref[0])
                def _():
                    body(start, length, i, tiles)

            return unused

        lax.fori_loop(0, tiles, one_tile, 0)
        return count + tiles

    lax.fori_loop(0, seq_count, one_seq, 0)


def forward_kernel(seq_count, slots, subs, split, place_ref, seq_ref, rank_ref, *refs):
    parts, outs, lse_ref, seq_out_ref, q_t, keys, v_t = refs
    tokens = slots * subs * BLK
    tail = q_t.shape[1] - tokens
    q_t[:, pl.ds(tokens, tail)] = jnp.zeros((HD, tail), bf16)
    v_t[:, pl.ds(tokens, tail)] = jnp.zeros((HD, tail), bf16)
    keys[pl.ds(tokens, tail), :] = jnp.zeros((tail, HD), bf16)
    if split > 1:
        lse_ref[...] = jnp.zeros(lse_ref.shape, f32)
        seq_out_ref[...] = jnp.zeros(seq_out_ref.shape, bf16)
    for s in range(slots):
        for b in range(subs):
            where = pl.multiple_of(place_ref[s * subs + b] * BLK, BLK)
            cols = slice(b * BLK, (b + 1) * BLK)
            q_t[:, pl.ds(where, BLK)] = parts[s, 0:HD, cols]
            keys[pl.ds(where, BLK), :] = flip(parts[s, HD : 2 * HD, cols])
            v_t[:, pl.ds(where, BLK)] = parts[s, 2 * HD :, cols]
    scale = HD ** (-0.5) * log2e
    row = lax.broadcasted_iota(jnp.int32, (TILE, TILE), 0)
    col = lax.broadcasted_iota(jnp.int32, (TILE, TILE), 1)

    def tile(start, length, i, tiles):
        q_at = pl.multiple_of(start + i * TILE, BLK)
        q_tile = q_t[:, pl.ds(q_at, TILE)]

        def step(j, carried, diagonal):
            run_max, run_sum, acc = carried
            k_at = pl.multiple_of(start + j * TILE, BLK)
            scores = dot_f32(keys[pl.ds(k_at, TILE), :], q_tile) * scale
            if diagonal:
                scores = jnp.where(row <= col, scores, masked_score)
            new_max = jnp.maximum(run_max, jnp.max(scores, axis=0, keepdims=True))
            factor = jnp.exp2(run_max - new_max)
            weights = jnp.exp2(scores - new_max)
            run_sum = run_sum * factor + jnp.sum(weights, axis=0, keepdims=True)
            acc = acc * factor + dot_f32(v_t[:, pl.ds(k_at, TILE)], weights.astype(bf16))
            return new_max, run_sum, acc

        carried = (
            jnp.full((1, TILE), masked_score, f32),
            jnp.zeros((1, TILE), f32),
            jnp.zeros((HD, TILE), f32),
        )
        carried = lax.fori_loop(0, i, lambda j, c: step(j, c, False), carried)
        run_max, run_sum, acc = step(i, carried, True)
        lse_ref[:, pl.ds(q_at, TILE)] = jnp.broadcast_to(run_max + jnp.log2(run_sum), (8, TILE))
        seq_out_ref[:, pl.ds(q_at, TILE)] = (acc / run_sum).astype(bf16)

    each_query_tile(seq_ref, rank_ref, seq_count, split, tile)
    for s in range(slots):
        for b in range(subs):
            where = pl.multiple_of(place_ref[s * subs + b] * BLK, BLK)
            outs[s, :, b * BLK : (b + 1) * BLK] = seq_out_ref[:, pl.ds(where, BLK)]


def backward_kernel(seq_count, slots, subs, split, place_ref, seq_ref, rank_ref, *refs):
    parts, grads, lse_ref, seq_out_ref, cos_ref, sin_ref, outs = refs[:7]
    k_t, q_up, g_down, kv, q_left, g_right, row_dot, dq_t, dkv = refs[7:]
    tokens = slots * subs * BLK
    tail = k_t.shape[1] - tokens
    q_up[HD:, :] = jnp.zeros((HD, tokens + tail), bf16)
    g_down[:HD, :] = jnp.zeros((HD, tokens + tail), bf16)
    k_t[:, pl.ds(tokens, tail)] = jnp.zeros((HD, tail), bf16)
    q_up[:HD, pl.ds(tokens, tail)] = jnp.zeros((HD, tail), bf16)
    g_down[HD:, pl.ds(tokens, tail)] = jnp.zeros((HD, tail), bf16)
    row_dot[:, pl.ds(tokens, tail)] = jnp.zeros((8, tail), f32)
    for wide in (kv, q_left, g_right):
        wide[pl.ds(tokens, tail), :] = jnp.zeros((tail, 2 * HD), bf16)
    dq_t[...] = jnp.zeros(dq_t.shape, f32)
    dkv[...] = jnp.zeros(dkv.shape, f32)
    left = lax.broadcasted_iota(jnp.int32, (BLK, 2 * HD), 1) < HD
    for s in range(slots):
        for b in range(subs):
            where = pl.multiple_of(place_ref[s * subs + b] * BLK, BLK)
            cols = slice(b * BLK, (b + 1) * BLK)
            at = pl.ds(where, BLK)
            q_blk = parts[s, 0:HD, cols]
            g_blk = grads[s, :, cols]
            q_up[:HD, at] = q_blk
            g_down[HD:, at] = g_blk
            k_t[:, at] = parts[s, HD : 2 * HD, cols]
            kv[at, :] = flip(parts[s, HD:, cols])
            both = jnp.transpose(jnp.concatenate([q_blk.astype(f32), g_blk.astype(f32)], axis=0))
            q_left[at, :] = jnp.where(left, both, 0.0).astype(bf16)
            g_right[at, :] = jnp.where(left, 0.0, both).astype(bf16)
            dots = jnp.sum(
                g_blk.astype(f32) * seq_out_ref[:, at].astype(f32), axis=0, keepdims=True
            )
            row_dot[:, at] = jnp.broadcast_to(dots, (8, BLK))
    scale = HD ** (-0.5)
    row = lax.broadcasted_iota(jnp.int32, (TILE, TILE), 0)
    col = lax.broadcasted_iota(jnp.int32, (TILE, TILE), 1)
    lane = lax.broadcasted_iota(jnp.int32, (1, TILE), 1)

    def pair(start, length, i, j, diagonal):
        q_at = pl.ds(pl.multiple_of(start + i * TILE, BLK), TILE)
        k_at = pl.ds(pl.multiple_of(start + j * TILE, BLK), TILE)
        lse = jnp.where(i * TILE + lane < length, lse_ref[0:1, q_at], far_score)
        kv_tile = kv[k_at, :]
        scores = dot_f32(kv_tile, q_up[:, q_at]) * (scale * log2e)
        if diagonal:
            scores = jnp.where(row <= col, scores, masked_score)
        probs = jnp.exp2(scores - lse)
        grad_probs = dot_f32(kv_tile, g_down[:, q_at])
        grad_scores = (probs * (grad_probs - row_dot[0:1, q_at])).astype(bf16)
        probs = probs.astype(bf16)
        dkv[k_at, :] += dot_f32(grad_scores, q_left[q_at, :]) + dot_f32(probs, g_right[q_at, :])
        return dot_f32(k_t[:, k_at], grad_scores)

    def tile(start, length, i, tiles):
        total = pair(start, length, i, i, True)
        total = lax.fori_loop(
            0, i, lambda j, c: c + pair(start, length, i, j, False), total
        )
        dq_t[:, pl.ds(pl.multiple_of(start + i * TILE, BLK), TILE)] = total

    each_query_tile(seq_ref, rank_ref, seq_count, split, tile)

    def unrotate(head_block, cosine, sine):
        lower = head_block[:HALF]
        upper = head_block[HALF:ROT]
        return jnp.concatenate(
            [
                lower * cosine + upper * sine,
                upper * cosine - lower * sine,
                head_block[ROT:],
            ],
            axis=0,
        )

    for s in range(slots):
        for b in range(subs):
            where = pl.multiple_of(place_ref[s * subs + b] * BLK, BLK)
            at = pl.ds(where, BLK)
            first = pl.multiple_of(place_ref[slots * subs + s * subs + b] * BLK, BLK)
            cosine = cos_ref[:, pl.ds(first, BLK)]
            sine = sin_ref[:, pl.ds(first, BLK)]
            cols = slice(b * BLK, (b + 1) * BLK)
            outs[s, 0:HD, cols] = unrotate(dq_t[:, at] * scale, cosine, sine).astype(bf16)
            pair_t = jnp.transpose(dkv[at, :])
            outs[s, HD : 2 * HD, cols] = unrotate(pair_t[:HD] * scale, cosine, sine).astype(bf16)
            outs[s, 2 * HD :, cols] = pair_t[HD:].astype(bf16)


def whole_vmem(count):
    return [pl.BlockSpec(memory_space=pltpu.VMEM)] * count


def attention_forward(place, seq, rank, parts, split):
    slots, unused, local_tokens = parts.shape
    tokens = slots * local_tokens
    padded = tokens + TILE
    pairs = tokens * tokens // 2
    return pl.pallas_call(
        functools.partial(forward_kernel, seq.shape[1], slots, local_tokens // BLK, split),
        name="attention_forward",
        out_shape=[
            jax.ShapeDtypeStruct((slots, HD, local_tokens), bf16),
            jax.ShapeDtypeStruct((8, padded), f32),
            jax.ShapeDtypeStruct((HD, padded), bf16),
        ],
        grid_spec=pltpu.PrefetchScalarGridSpec(
            num_scalar_prefetch=3,
            grid=(),
            in_specs=whole_vmem(1),
            out_specs=whole_vmem(3),
            scratch_shapes=[
                pltpu.VMEM((HD, padded), bf16),
                pltpu.VMEM((padded, HD), bf16),
                pltpu.VMEM((HD, padded), bf16),
            ],
        ),
        compiler_params=pltpu.CompilerParams(vmem_limit_bytes=60 * 2**20),
        cost_estimate=pl.CostEstimate(
            flops=16 * pairs * HD, bytes_accessed=tokens * HD * 12, transcendentals=pairs
        ),
    )(place, seq, rank, parts)


def attention_backward(place, seq, rank, parts, grads, lse, seq_out, cosine, sine, split):
    slots, unused, local_tokens = parts.shape
    tokens = slots * local_tokens
    padded = tokens + TILE
    pairs = tokens * tokens // 2
    return pl.pallas_call(
        functools.partial(backward_kernel, seq.shape[1], slots, local_tokens // BLK, split),
        name="attention_backward",
        out_shape=jax.ShapeDtypeStruct((slots, 3 * HD, local_tokens), bf16),
        grid_spec=pltpu.PrefetchScalarGridSpec(
            num_scalar_prefetch=3,
            grid=(),
            in_specs=whole_vmem(6),
            out_specs=whole_vmem(1)[0],
            scratch_shapes=[
                pltpu.VMEM((HD, padded), bf16),
                pltpu.VMEM((2 * HD, padded), bf16),
                pltpu.VMEM((2 * HD, padded), bf16),
                pltpu.VMEM((padded, 2 * HD), bf16),
                pltpu.VMEM((padded, 2 * HD), bf16),
                pltpu.VMEM((padded, 2 * HD), bf16),
                pltpu.VMEM((8, padded), f32),
                pltpu.VMEM((HD, padded), f32),
                pltpu.VMEM((padded, 2 * HD), f32),
            ],
        ),
        compiler_params=pltpu.CompilerParams(vmem_limit_bytes=62 * 2**20),
        cost_estimate=pl.CostEstimate(
            flops=40 * pairs * HD, bytes_accessed=tokens * HD * 24, transcendentals=pairs
        ),
    )(place, seq, rank, parts, grads, lse, seq_out, cosine, sine)


def swap(value, axis, size, offset):
    return lax.ppermute(value, axis, [(i, i ^ offset) for i in range(size)])


def axis_bits(size):
    return [1 << k for k in range(size.bit_length() - 1)]


def all_sum(value, axis, size):
    for bit in axis_bits(size):
        value = value + swap(value, axis, size, bit)
    return value


def slot_order(bits):
    if not bits:
        return [0]
    rest = slot_order(bits[1:])
    return [s | bits[0] for s in rest] + rest


def product_kernel(dims, tiles, orders, table_ref, *refs):
    step = pl.program_id(0)
    count = len(orders[0])
    pieces = [refs[k * (count + 1) : k * (count + 1) + count] for k in range(len(dims))]
    factors = [refs[k * (count + 1) + count] for k in range(len(dims))]
    refs = refs[len(dims) * (count + 1) :]
    refs, stacks = refs[: -len(dims)], refs[-len(dims) :]

    @pl.when(step == 0)
    def _():
        for stack, parts, (lhs_dim, unused) in zip(stacks, pieces, dims):
            rows = parts[0].shape[1 - lhs_dim]
            for p, part in enumerate(parts):
                if lhs_dim == 0:
                    stack[:, p * rows : (p + 1) * rows] = part[...]
                else:
                    stack[p * rows : (p + 1) * rows, :] = part[...]

    at = 0
    for stack, factor, (lhs_dim, rhs_dim) in zip(stacks, factors, dims):
        product = lax.dot_general(
            stack[...],
            factor[...],
            (((lhs_dim,), (rhs_dim,)), ((), ())),
            preferred_element_type=f32,
        )
        columns = slice(at, at + product.shape[1])
        at += product.shape[1]
        if len(refs) == 1:
            refs[0][:, columns] = product.astype(bf16)
            continue
        added, outs = refs[0], refs[1:]
        product = (product + added[:, columns].astype(f32)).astype(bf16)
        rows = product.shape[0] // count
        for half, order in enumerate(orders):

            @pl.when(step // tiles == half)
            def _(half=half, order=order, product=product, columns=columns, rows=rows):
                for p, slot in enumerate(order):
                    source = orders[0].index(slot)
                    out = outs[2 * half + p // (count // 2)]
                    first = p % (count // 2) * rows
                    out[first : first + rows, columns] = product[
                        source * rows : (source + 1) * rows
                    ]


def piece_products(owners, size, pairs, orders, added):
    count = len(orders[0])
    tiles = 2 if len(pairs) == 1 else 1
    in_specs, operands, scratch, width, flops = [], [], [], 0, 0
    for lhs, rhs, lhs_dim, rhs_dim in pairs:
        tokens = lhs.shape[lhs_dim]
        rows = lhs.shape[1 - lhs_dim] // size
        columns = rhs.shape[1 - rhs_dim] // (2 * tiles)
        width += columns
        flops += 4 * tiles * count * rows * columns * tokens
        for p in range(count):
            if lhs_dim == 0:
                in_specs.append(pl.BlockSpec((tokens, rows), lambda i, t, p=p: (0, t[p])))
            else:
                in_specs.append(pl.BlockSpec((rows, tokens), lambda i, t, p=p: (t[p], 0)))
            operands.append(lhs)
        if rhs_dim == 0:
            in_specs.append(pl.BlockSpec((tokens, columns), lambda i, t: (0, i)))
        else:
            in_specs.append(pl.BlockSpec((columns, tokens), lambda i, t: (i, 0)))
        operands.append(rhs)
        stack = (tokens, count * rows) if lhs_dim == 0 else (count * rows, tokens)
        scratch.append(pltpu.VMEM(stack, bf16))
    if added is None:
        out_shape = [jax.ShapeDtypeStruct((count * rows, 2 * tiles * width), bf16)]
        out_specs = [pl.BlockSpec((count * rows, width), lambda i, t: (0, i))]
    else:
        in_specs.append(pl.BlockSpec((count * rows, width), lambda i, t: (0, i)))
        operands.append(added)
        out_shape = [jax.ShapeDtypeStruct((count // 2 * rows, tiles * width), bf16)] * 4
        out_specs = [
            pl.BlockSpec(
                (count // 2 * rows, width),
                lambda i, t, at=half * tiles: (0, jnp.clip(i - at, 0, tiles - 1)),
            )
            for half in (0, 0, 1, 1)
        ]
    dims = [(lhs_dim, rhs_dim) for unused, unused_too, lhs_dim, rhs_dim in pairs]
    return pl.pallas_call(
        functools.partial(product_kernel, dims, tiles, orders),
        name="piece_products",
        out_shape=out_shape,
        grid_spec=pltpu.PrefetchScalarGridSpec(
            num_scalar_prefetch=1,
            grid=(2 * tiles,),
            in_specs=in_specs,
            out_specs=out_specs,
            scratch_shapes=scratch,
        ),
        compiler_params=pltpu.CompilerParams(vmem_limit_bytes=52 * 2**20),
        cost_estimate=pl.CostEstimate(
            flops=flops,
            bytes_accessed=4 * tiles * width * (2 * count * rows + tokens),
            transcendentals=0,
        ),
    )(owners.astype(jnp.int32), *operands)


def halves_orders(size):
    upper = axis_bits(size)[1:]
    return [(upper, slot_order(upper)), (upper[::-1], slot_order(upper[::-1]))]


def tie(*values):
    return lax.optimization_barrier(values)


class PieceSum:
    def __init__(self, index, size, *pairs):
        self.index, self.size = index, size
        self.orders = halves_orders(size)
        self.bits = [bits for bits, unused in self.orders]
        self.pairs = pairs
        self.spreading = self.finished = False

    def swaps(self, values):
        bits = [half[self.level] for half in self.bits]
        self.pending = [swap(v, "dp", self.size, bit) for v, bit in zip(values, bits)]

    def across_cores(self):
        far = self.index ^ jnp.array([s | 1 for s in self.orders[0][1]], jnp.int32)
        orders = [order for unused, order in self.orders]
        self.kept = piece_products(far, self.size, self.pairs, orders, None)
        self.pending = [swap(self.kept[0], "dp", self.size, 1)]

    def products(self):
        near = self.index ^ jnp.array(self.orders[0][1], jnp.int32)
        orders = [order for unused, order in self.orders]
        made = piece_products(near, self.size, self.pairs, orders, self.pending[0])
        sends, self.kept = [made[0], made[2]], [made[1], made[3]]
        self.level = 0
        self.swaps(sends)

    def advance(self):
        if self.spreading:
            self.advance_spread()
            return
        self.level += 1
        if self.level < len(self.bits[0]):
            sends, keeps = [], []
            for keep, got in zip(self.kept, self.pending):
                cut = keep.shape[0] // 2
                sends.append((keep[:cut].astype(f32) + got[:cut].astype(f32)).astype(bf16))
                keeps.append((keep[cut:].astype(f32) + got[cut:].astype(f32)).astype(bf16))
            self.kept = keeps
            self.swaps(sends)
            return
        self.kept = [
            (keep.astype(f32) + got.astype(f32)).astype(bf16)
            for keep, got in zip(self.kept, self.pending)
        ]
        self.slots = [[0], [0]]
        self.spreading = True
        self.level -= 1
        self.swaps(self.kept)

    def advance_spread(self):
        if self.level > 0:
            self.kept = [jnp.concatenate(p, axis=0) for p in zip(self.kept, self.pending)]
            self.slots = [
                have + [s | half[self.level] for s in have]
                for have, half in zip(self.slots, self.bits)
            ]
            self.level -= 1
            self.swaps(self.kept)
        elif self.level == 0:
            self.others = self.pending
            self.level = -1
            self.pending = [swap(v, "dp", self.size, 1) for v in self.kept + self.others]
        else:
            self.finished = True

    def spread(self, *layout):
        while not self.finished:
            arrived([self])
            self.advance()
        arrays, slots = [], []
        for h in range(2):
            have = self.slots[h]
            other = [s | self.bits[h][0] for s in have]
            arrays += [self.kept[h], self.others[h], self.pending[h], self.pending[h + 2]]
            slots += have + other + [s | 1 for s in have + other]
        return spread(self.index, self.size, arrays, slots, layout)


def arrived(sums, *values):
    count = [len(s.pending) for s in sums]
    out = list(tie(*[p for s in sums for p in s.pending], *values))
    for s, n in zip(sums, count):
        s.pending, out = out[:n], out[n:]
    return out


def computed(sums, *values):
    count = [len(s.kept) for s in sums]
    out = list(tie(*[p for s in sums for p in s.kept], *values))
    for s, n in zip(sums, count):
        s.kept, out = out[:n], out[n:]
    return out


def spread_kernel(quarter, layout, table_ref, *refs):
    ins, outs = refs[:8], refs[8:]
    step = pl.program_id(0)
    for j, piece in enumerate(ins):

        @pl.when(step // quarter == j)
        def _(piece=piece):
            at = 0
            for out, (parts, columns, transposed) in zip(outs, layout):
                for c in range(parts):
                    block = piece[:, at : at + columns].astype(f32)
                    at += columns
                    if parts > 1:
                        out[c] = block
                    else:
                        out[...] = jnp.transpose(block) if transposed else block


def spread(index, size, arrays, slots, layout):
    table = index ^ jnp.array(slots, jnp.int32)
    quarter = size // 4
    rows, width = arrays[0].shape[0] // quarter, arrays[0].shape[1]
    in_specs = [
        pl.BlockSpec(
            (rows, width),
            lambda i, t, at=j * quarter: (jnp.clip(i - at, 0, quarter - 1), 0),
        )
        for j in range(8)
    ]
    out_shape, out_specs = [], []
    for parts, columns, transposed in layout:
        if parts > 1:
            out_shape.append((parts, rows * size, 2 * columns))
            out_specs.append(
                pl.BlockSpec((parts, rows, columns), lambda i, t: (0, t[i], i // size))
            )
        elif transposed:
            out_shape.append((2 * columns, rows * size))
            out_specs.append(pl.BlockSpec((columns, rows), lambda i, t: (i // size, t[i])))
        else:
            out_shape.append((rows * size, 2 * columns))
            out_specs.append(pl.BlockSpec((rows, columns), lambda i, t: (t[i], i // size)))
    return pl.pallas_call(
        functools.partial(spread_kernel, quarter, layout),
        name="spread",
        out_shape=[jax.ShapeDtypeStruct(shape, f32) for shape in out_shape],
        grid_spec=pltpu.PrefetchScalarGridSpec(
            num_scalar_prefetch=1, grid=(2 * size,), in_specs=in_specs, out_specs=out_specs
        ),
        compiler_params=pltpu.CompilerParams(vmem_limit_bytes=48 * 2**20),
        cost_estimate=pl.CostEstimate(
            flops=0, bytes_accessed=rows * width * size * 12, transcendentals=0
        ),
    )(table, *arrays)


def local(
    dp_size,
    hidden_in,
    gain,
    bias,
    w_qkv,
    b_qkv,
    w_dense,
    b_dense,
    w_fc1,
    b_fc1,
    w_fc2,
    b_fc2,
    cotangent,
    seq_lengths,
    padding,
    block_perm,
):
    tok_local, dim_local = hidden_in.shape
    model_width = gain.shape[0]
    heads = w_qkv.shape[2] // HD
    split = dp_size // heads
    subs = tok_local // BLK
    nblk = block_perm.shape[0]
    data_index = lax.axis_index("dp")
    tensor_index = lax.axis_index("tensor")
    pos_all, valid_all = token_table(seq_lengths, padding, block_perm)
    my_pos = lax.dynamic_slice_in_dim(pos_all, data_index * tok_local, tok_local)
    my_valid = lax.dynamic_slice_in_dim(valid_all, data_index * tok_local, tok_local)
    cosine, sine = rotary_tables(my_pos)
    cosine_all, sine_all = rotary_tables(jnp.arange(nblk * BLK, dtype=jnp.int32))
    place = jnp.concatenate([block_perm, pos_all[::BLK] // BLK])
    seq = jnp.stack([jnp.cumsum(seq_lengths) - seq_lengths, seq_lengths])
    rank = (data_index // heads).reshape(1).astype(jnp.int32)

    def to_heads(stacked):
        stacked = jnp.concatenate([stacked] * split) if split > 1 else stacked
        return lax.all_to_all(stacked, "dp", 0, 0, tiled=True)

    def to_tokens(stacked):
        got = lax.all_to_all(stacked, "dp", 0, 0, tiled=True)
        if split > 1:
            got = got.reshape(split, heads, *got.shape[1:]).astype(f32)
            got = jnp.sum(got, axis=0).astype(bf16)
        return got

    full_in = lax.all_gather(hidden_in.astype(bf16), "tensor", axis=1, tiled=True)
    grad_proj = lax.all_gather(cotangent.astype(bf16), "tensor", axis=1, tiled=True)
    w_back = row_major(jnp.transpose(w_qkv, (1, 2, 0)))
    full_in, w_back, cosine, sine, cosine_all, sine_all, place, seq = tie(
        full_in, w_back, cosine, sine, cosine_all, sine_all, place, seq
    )
    full_in = full_in.astype(f32)
    row_mean = jnp.mean(full_in, axis=-1, keepdims=True)
    centered = full_in - row_mean
    inv_std = lax.rsqrt(jnp.mean(centered * centered, axis=-1, keepdims=True) + epsilon)
    normal_x = centered * inv_std
    normed = (normal_x * gain + bias).astype(bf16)
    projections = (
        jnp.einsum("td,dcf->cft", normed, w_qkv, preferred_element_type=f32) + b_qkv[:, :, None]
    ).reshape(3, heads, HD, tok_local)
    turned = projections[:2, :, :ROT].reshape(2, heads, 2, HALF, tok_local)
    lower, upper = turned[:, :, 0], turned[:, :, 1]
    rotated = jnp.concatenate(
        [
            lower * cosine - upper * sine,
            upper * cosine + lower * sine,
            projections[:2, :, ROT:],
        ],
        axis=2,
    )
    packed = jnp.concatenate([rotated[0], rotated[1], projections[2]], axis=1).astype(bf16)
    parts = to_heads(packed)
    hidden_pre = jnp.dot(normed, w_fc1, preferred_element_type=f32) + b_fc1
    activated = gelu_tanh(hidden_pre).astype(bf16)
    activated_t, normed_t = row_major(jnp.transpose(activated)), row_major(jnp.transpose(normed))
    parts, hidden_pre, activated, activated_t, normed_t, grad_proj = tie(
        parts, hidden_pre, activated, activated_t, normed_t, grad_proj
    )

    def new_sum(*pairs):
        made = PieceSum(data_index, dp_size, *pairs)
        made.across_cores()
        return made

    sum_fc2 = new_sum((activated_t, grad_proj, 1, 0))
    (grad_proj,) = computed([sum_fc2], grad_proj)
    grad_attended = jnp.einsum(
        "ed,td->et", w_dense, grad_proj, preferred_element_type=f32
    ).astype(bf16)
    (grad_attended,) = arrived([sum_fc2], grad_attended)
    grad_stack = to_heads(grad_attended.reshape(heads, HD, tok_local))
    sum_fc2.products()
    grad_proj, hidden_pre = computed([sum_fc2], grad_proj, hidden_pre)
    grad_act = jnp.einsum("td,fd->tf", grad_proj, w_fc2, preferred_element_type=f32)
    unused_value, gelu_back = jax.vjp(gelu_tanh, hidden_pre)
    grad_hidden = gelu_back(grad_act)[0].astype(bf16)
    (grad_hidden,) = arrived([sum_fc2], grad_hidden)
    sum_fc1 = new_sum((normed_t, grad_hidden, 1, 0))
    sum_fc1.kept = arrived([sum_fc1], *sum_fc1.kept)
    sum_fc2.advance()
    sum_fc1.pending = computed([sum_fc2], *sum_fc1.pending)
    sum_fc1.products()

    (parts,) = computed([sum_fc2, sum_fc1], parts)
    out_stack, lse, seq_out = attention_forward(place, seq, rank, parts, split)
    out_stack, grad_stack, lse = arrived([sum_fc2, sum_fc1], out_stack, grad_stack, lse)
    attended = to_tokens(out_stack).reshape(heads * HD, tok_local)
    sum_fc2.advance()
    sum_fc1.advance()
    (lse,) = computed([sum_fc2, sum_fc1], lse)
    grad_pieces = attention_backward(
        place, seq, rank, parts, grad_stack, lse, seq_out, cosine_all, sine_all, split
    )
    grad_pieces, attended, grad_hidden, activated = arrived(
        [sum_fc2, sum_fc1], grad_pieces, attended, grad_hidden, activated
    )

    grad_qkv = to_tokens(grad_pieces).reshape(heads, 3, HD, tok_local)
    partial_value = jnp.einsum(
        "et,ed->td", attended, w_dense, preferred_element_type=f32
    ) + jnp.dot(activated, w_fc2, preferred_element_type=f32)
    partial_value = partial_value.astype(bf16)
    projected = lax.psum_scatter(
        partial_value, "tensor", scatter_dimension=1, tiled=True
    ).astype(f32)
    grad_normed = jnp.einsum("tf,df->td", grad_hidden, w_fc1, preferred_element_type=f32)
    grad_qkv, grad_normed, partial_value, *waiting = tie(
        grad_qkv, grad_normed, partial_value, *sum_fc2.pending, *sum_fc1.pending
    )
    sum_fc2.pending, sum_fc1.pending = waiting[:2], waiting[2:]
    sum_fc2.advance()
    sum_fc1.advance()
    branch = projected + b_dense + b_fc2
    output = hidden_in + branch
    valid_rows = my_valid.astype(f32)[:, None]
    sum_output = jnp.sum(output * output * valid_rows)
    sum_branch = jnp.sum(branch * branch * valid_rows)
    valid_count = jnp.sum(valid_all.astype(f32)) * model_width

    grad_b_fc1 = jnp.sum(grad_hidden.astype(f32), axis=0)
    grad_b_qkv = jnp.transpose(jnp.sum(grad_qkv.astype(f32), axis=3), (1, 0, 2))
    by_half = jnp.transpose(
        grad_qkv.reshape(2, heads // 2, 3, HD, tok_local), (0, 2, 1, 3, 4)
    ).reshape(3 * heads * HD, tok_local)
    sum_qkv = new_sum((normed_t, by_half, 1, 1), (grad_proj, attended, 0, 1))
    (grad_qkv,) = computed([sum_qkv], grad_qkv)
    grad_normed = row_major(
        grad_normed
        + jnp.einsum(
            "hcet,ched->td",
            grad_qkv,
            w_back.reshape(3, heads, HD, model_width),
            preferred_element_type=f32,
        )
    )
    grad_narrow = grad_normed.astype(bf16)
    (grad_narrow,) = arrived([sum_qkv, sum_fc2], grad_narrow)
    grad_local = lax.psum_scatter(
        grad_narrow, "tensor", scatter_dimension=1, tiled=True
    ).astype(f32)
    sum_qkv.products()
    sum_qkv.kept = arrived([sum_fc1], *sum_qkv.kept)
    sum_fc2.advance()
    sum_fc1.advance()
    sum_fc2.pending = computed([sum_qkv], *sum_fc2.pending)
    (grad_w_fc2,) = sum_fc2.spread((1, model_width // 2, False))
    (grad_w_fc2,) = arrived([sum_fc1, sum_qkv], grad_w_fc2)
    sum_fc1.advance()
    sum_qkv.advance()
    scaled = grad_normed * gain
    mean_sums = jnp.stack([jnp.sum(scaled, axis=1), jnp.sum(scaled * normal_x, axis=1)])
    shared = jnp.concatenate([mean_sums.reshape(-1), sum_output[None], sum_branch[None]])
    sum_fc1.pending = computed([sum_qkv], *sum_fc1.pending)
    sum_fc1.advance()
    (grad_w_fc1,) = sum_fc1.spread((1, w_fc1.shape[1] // 2, False))
    grad_w_fc1, shared = arrived([sum_qkv], grad_w_fc1, shared)
    sum_qkv.advance()
    shared = all_sum(shared, "tensor", model_width // dim_local)
    mean_sums = shared[:-2].reshape(2, tok_local) / model_width
    mean_one, mean_two = mean_sums[0][:, None], mean_sums[1][:, None]
    gain_local = lax.dynamic_slice_in_dim(gain, tensor_index * dim_local, dim_local)
    normal_local = lax.dynamic_slice_in_dim(normal_x, tensor_index * dim_local, dim_local, 1)
    grad_input = cotangent + inv_std * (
        grad_local * gain_local - mean_one - normal_local * mean_two
    )
    late = jnp.concatenate(
        [
            jnp.sum(grad_local * normal_local, axis=0),
            jnp.sum(grad_local, axis=0),
            jnp.sum(cotangent, axis=0),
            grad_b_fc1,
            grad_b_qkv.reshape(-1),
            shared[-2:],
        ]
    )
    cuts = [dim_local, 2 * dim_local, 3 * dim_local, 3 * dim_local + grad_b_fc1.shape[0]]
    late = all_sum(late, "dp", dp_size)
    while not sum_qkv.finished:
        arrived([sum_qkv])
        sum_qkv.advance()
    sum_qkv.pending[0], late = tie(sum_qkv.pending[0], late)
    grad_w_qkv, grad_w_dense = sum_qkv.spread(
        (3, heads * HD // 2, False), (1, heads * HD // 2, True)
    )
    grad_w_qkv = jnp.transpose(grad_w_qkv, (1, 0, 2))
    totals = late[-2:]
    rms = jnp.sqrt(totals / valid_count)
    bias_grad = late[cuts[1] : cuts[2]]
    return (
        output,
        grad_input,
        late[: cuts[0]],
        late[cuts[0] : cuts[1]],
        grad_w_qkv,
        late[cuts[3] : -2].reshape(3, heads * HD),
        grad_w_dense,
        bias_grad,
        grad_w_fc1,
        late[cuts[2] : cuts[3]],
        grad_w_fc2,
        bias_grad,
        rms[0],
        rms[1],
    )


def solution(mesh):
    return jax.shard_map(
        functools.partial(local, mesh.shape["dp"]),
        mesh=mesh,
        in_specs=(
            P("dp", "tensor"),
            P(),
            P(),
            P(None, None, "tensor"),
            P(None, "tensor"),
            P("tensor", None),
            P("tensor"),
            P(None, "tensor"),
            P("tensor"),
            P("tensor", None),
            P("tensor"),
            P("dp", "tensor"),
            P(),
            P(),
            P(),
        ),
        out_specs=(
            P("dp", "tensor"),
            P("dp", "tensor"),
            P("tensor"),
            P("tensor"),
            P(None, None, "tensor"),
            P(None, "tensor"),
            P("tensor", None),
            P("tensor"),
            P(None, "tensor"),
            P("tensor"),
            P("tensor", None),
            P("tensor"),
            P(),
            P(),
        ),
        check_vma=False,
    )
```

```python
import functools

import jax
import jax.numpy as jnp
from jax import lax
from jax.experimental import pallas as pl
from jax.experimental.layout import Layout, with_layout_constraint
from jax.experimental.pallas import tpu as pltpu
from jax.sharding import PartitionSpec as P

HD = 64
ROT = 32
HALF = ROT // 2
BLK = 128
TILE = 512

epsilon = 1e-05
masked_score = -1e30
far_score = 1e30
log2e = 1.4426950408889634
f32 = jnp.float32
bf16 = jnp.bfloat16


def row_major(value):
    return with_layout_constraint(value, Layout(tuple(range(value.ndim))))


def token_table(seq_lengths, padding, initial):
    seq_count = seq_lengths.shape[0]
    seq_ends = jnp.cumsum(seq_lengths)
    seq_starts = seq_ends - seq_lengths
    seq_block = jnp.sum((initial[:, None] >= seq_ends[None, :]).astype(jnp.int32), axis=1)
    members = (seq_block[:, None] == jnp.arange(seq_count, dtype=jnp.int32)[None, :]).astype(
        jnp.int32
    )
    first_block = jnp.sum(members * seq_starts[None, :], axis=1)
    limits = jnp.sum(members * (seq_lengths * BLK - padding)[None, :], axis=1)
    offsets = jnp.arange(BLK, dtype=jnp.int32)
    positions = (initial - first_block)[:, None] * BLK + offsets[None, :]
    is_valid = positions < limits[:, None]
    return (positions.reshape(-1), is_valid.reshape(-1))


def rotary_tables(positions):
    frequency = 10000.0 ** (-jnp.arange(0, ROT, 2, dtype=f32) / ROT)
    angles = frequency[:, None] * positions.astype(f32)[None, :]
    return (jnp.cos(angles), jnp.sin(angles))


def gelu_tanh(gelu_input):
    return jax.nn.gelu(gelu_input, approximate=True)


def dot_f32(a, b):
    return lax.dot_general(a, b, (((1,), (0,)), ((), ())), preferred_element_type=f32)


def flip(block):
    return jnp.transpose(block.astype(f32)).astype(bf16)


def each_query_tile(seq_ref, rank_ref, seq_count, split, body):
    def one_seq(s, count):
        start = seq_ref[0, s] * BLK
        length = seq_ref[1, s] * BLK
        tiles = (length + TILE - 1) // TILE

        def one_tile(i, unused):
            if split == 1:
                body(start, length, i, tiles)
            else:

                @pl.when(lax.rem(count + i, split) == rank_ref[0])
                def _():
                    body(start, length, i, tiles)

            return unused

        lax.fori_loop(0, tiles, one_tile, 0)
        return count + tiles

    lax.fori_loop(0, seq_count, one_seq, 0)


def forward_kernel(seq_count, slots, subs, split, place_ref, seq_ref, rank_ref, *refs):
    parts, outs, lse_ref, seq_out_ref, q_t, keys, v_t = refs
    tokens = slots * subs * BLK
    tail = q_t.shape[1] - tokens
    q_t[:, pl.ds(tokens, tail)] = jnp.zeros((HD, tail), bf16)
    v_t[:, pl.ds(tokens, tail)] = jnp.zeros((HD, tail), bf16)
    keys[pl.ds(tokens, tail), :] = jnp.zeros((tail, HD), bf16)
    if split > 1:
        lse_ref[...] = jnp.zeros(lse_ref.shape, f32)
        seq_out_ref[...] = jnp.zeros(seq_out_ref.shape, bf16)
    @pl.loop(0, slots)
    def _(s):
        for b in range(subs):
            where = pl.multiple_of(place_ref[s * subs + b] * BLK, BLK)
            cols = slice(b * BLK, (b + 1) * BLK)
            q_t[:, pl.ds(where, BLK)] = parts[s, 0:HD, cols]
            keys[pl.ds(where, BLK), :] = flip(parts[s, HD : 2 * HD, cols])
            v_t[:, pl.ds(where, BLK)] = parts[s, 2 * HD :, cols]
    scale = HD ** (-0.5) * log2e
    row = lax.broadcasted_iota(jnp.int32, (TILE, TILE), 0)
    col = lax.broadcasted_iota(jnp.int32, (TILE, TILE), 1)

    def tile(start, length, i, tiles):
        q_at = pl.multiple_of(start + i * TILE, BLK)
        q_tile = q_t[:, pl.ds(q_at, TILE)]

        def step(j, carried, diagonal):
            run_max, run_sum, acc = carried
            k_at = pl.multiple_of(start + j * TILE, BLK)
            scores = dot_f32(keys[pl.ds(k_at, TILE), :], q_tile) * scale
            if diagonal:
                scores = jnp.where(row <= col, scores, masked_score)
            new_max = jnp.maximum(run_max, jnp.max(scores, axis=0, keepdims=True))
            factor = jnp.exp2(run_max - new_max)
            weights = jnp.exp2(scores - new_max)
            run_sum = run_sum * factor + jnp.sum(weights, axis=0, keepdims=True)
            acc = acc * factor + dot_f32(v_t[:, pl.ds(k_at, TILE)], weights.astype(bf16))
            return new_max, run_sum, acc

        carried = (
            jnp.full((1, TILE), masked_score, f32),
            jnp.zeros((1, TILE), f32),
            jnp.zeros((HD, TILE), f32),
        )
        carried = lax.fori_loop(0, i, lambda j, c: step(j, c, False), carried)
        run_max, run_sum, acc = step(i, carried, True)
        lse_ref[:, pl.ds(q_at, TILE)] = jnp.broadcast_to(run_max + jnp.log2(run_sum), (8, TILE))
        seq_out_ref[:, pl.ds(q_at, TILE)] = (acc / run_sum).astype(bf16)

    each_query_tile(seq_ref, rank_ref, seq_count, split, tile)
    @pl.loop(0, slots)
    def _(s):
        for b in range(subs):
            where = pl.multiple_of(place_ref[s * subs + b] * BLK, BLK)
            outs[s, :, b * BLK : (b + 1) * BLK] = seq_out_ref[:, pl.ds(where, BLK)]


def backward_kernel(seq_count, slots, subs, split, place_ref, seq_ref, rank_ref, *refs):
    parts, grads, lse_ref, seq_out_ref, cos_ref, sin_ref, outs = refs[:7]
    k_t, q_up, g_down, kv, q_left, g_right, row_dot, dq_t, dkv = refs[7:]
    tokens = slots * subs * BLK
    tail = k_t.shape[1] - tokens
    q_up[HD:, :] = jnp.zeros((HD, tokens + tail), bf16)
    g_down[:HD, :] = jnp.zeros((HD, tokens + tail), bf16)
    k_t[:, pl.ds(tokens, tail)] = jnp.zeros((HD, tail), bf16)
    q_up[:HD, pl.ds(tokens, tail)] = jnp.zeros((HD, tail), bf16)
    g_down[HD:, pl.ds(tokens, tail)] = jnp.zeros((HD, tail), bf16)
    row_dot[:, pl.ds(tokens, tail)] = jnp.zeros((8, tail), f32)
    for wide in (kv, q_left, g_right):
        wide[pl.ds(tokens, tail), :] = jnp.zeros((tail, 2 * HD), bf16)
    dq_t[...] = jnp.zeros(dq_t.shape, f32)
    dkv[...] = jnp.zeros(dkv.shape, f32)
    left = lax.broadcasted_iota(jnp.int32, (BLK, 2 * HD), 1) < HD
    @pl.loop(0, slots)
    def _(s):
        for b in range(subs):
            where = pl.multiple_of(place_ref[s * subs + b] * BLK, BLK)
            cols = slice(b * BLK, (b + 1) * BLK)
            at = pl.ds(where, BLK)
            q_blk = parts[s, 0:HD, cols]
            g_blk = grads[s, :, cols]
            q_up[:HD, at] = q_blk
            g_down[HD:, at] = g_blk
            k_t[:, at] = parts[s, HD : 2 * HD, cols]
            kv[at, :] = flip(parts[s, HD:, cols])
            both = jnp.transpose(jnp.concatenate([q_blk.astype(f32), g_blk.astype(f32)], axis=0))
            q_left[at, :] = jnp.where(left, both, 0.0).astype(bf16)
            g_right[at, :] = jnp.where(left, 0.0, both).astype(bf16)
            dots = jnp.sum(
                g_blk.astype(f32) * seq_out_ref[:, at].astype(f32), axis=0, keepdims=True
            )
            row_dot[:, at] = jnp.broadcast_to(dots, (8, BLK))
    scale = HD ** (-0.5)
    row = lax.broadcasted_iota(jnp.int32, (TILE, TILE), 0)
    col = lax.broadcasted_iota(jnp.int32, (TILE, TILE), 1)
    lane = lax.broadcasted_iota(jnp.int32, (1, TILE), 1)

    def pair(start, length, i, j, diagonal):
        q_at = pl.ds(pl.multiple_of(start + i * TILE, BLK), TILE)
        k_at = pl.ds(pl.multiple_of(start + j * TILE, BLK), TILE)
        lse = jnp.where(i * TILE + lane < length, lse_ref[0:1, q_at], far_score)
        kv_tile = kv[k_at, :]
        scores = dot_f32(kv_tile, q_up[:, q_at]) * (scale * log2e)
        if diagonal:
            scores = jnp.where(row <= col, scores, masked_score)
        probs = jnp.exp2(scores - lse)
        grad_probs = dot_f32(kv_tile, g_down[:, q_at])
        grad_scores = (probs * (grad_probs - row_dot[0:1, q_at])).astype(bf16)
        probs = probs.astype(bf16)
        dkv[k_at, :] += dot_f32(grad_scores, q_left[q_at, :]) + dot_f32(probs, g_right[q_at, :])
        return dot_f32(k_t[:, k_at], grad_scores)

    def tile(start, length, i, tiles):
        total = pair(start, length, i, i, True)
        total = lax.fori_loop(
            0, i, lambda j, c: c + pair(start, length, i, j, False), total
        )
        dq_t[:, pl.ds(pl.multiple_of(start + i * TILE, BLK), TILE)] = total

    each_query_tile(seq_ref, rank_ref, seq_count, split, tile)

    def unrotate(head_block, cosine, sine):
        lower = head_block[:HALF]
        upper = head_block[HALF:ROT]
        return jnp.concatenate(
            [
                lower * cosine + upper * sine,
                upper * cosine - lower * sine,
                head_block[ROT:],
            ],
            axis=0,
        )

    @pl.loop(0, slots)
    def _(s):
        for b in range(subs):
            where = pl.multiple_of(place_ref[s * subs + b] * BLK, BLK)
            at = pl.ds(where, BLK)
            first = pl.multiple_of(place_ref[slots * subs + s * subs + b] * BLK, BLK)
            cosine = cos_ref[:, pl.ds(first, BLK)]
            sine = sin_ref[:, pl.ds(first, BLK)]
            cols = slice(b * BLK, (b + 1) * BLK)
            outs[s, 0:HD, cols] = unrotate(dq_t[:, at] * scale, cosine, sine).astype(bf16)
            pair_t = jnp.transpose(dkv[at, :])
            outs[s, HD : 2 * HD, cols] = unrotate(pair_t[:HD] * scale, cosine, sine).astype(bf16)
            outs[s, 2 * HD :, cols] = pair_t[HD:].astype(bf16)


def whole_vmem(count):
    return [pl.BlockSpec(memory_space=pltpu.VMEM)] * count


def attention_forward(place, seq, rank, parts, split):
    slots, unused, local_tokens = parts.shape
    tokens = slots * local_tokens
    padded = tokens + TILE
    pairs = tokens * tokens // 2
    return pl.pallas_call(
        functools.partial(forward_kernel, seq.shape[1], slots, local_tokens // BLK, split),
        name="attention_forward",
        out_shape=[
            jax.ShapeDtypeStruct((slots, HD, local_tokens), bf16),
            jax.ShapeDtypeStruct((8, padded), f32),
            jax.ShapeDtypeStruct((HD, padded), bf16),
        ],
        grid_spec=pltpu.PrefetchScalarGridSpec(
            num_scalar_prefetch=3,
            grid=(),
            in_specs=whole_vmem(1),
            out_specs=whole_vmem(3),
            scratch_shapes=[
                pltpu.VMEM((HD, padded), bf16),
                pltpu.VMEM((padded, HD), bf16),
                pltpu.VMEM((HD, padded), bf16),
            ],
        ),
        compiler_params=pltpu.CompilerParams(vmem_limit_bytes=60 * 2**20),
        cost_estimate=pl.CostEstimate(
            flops=16 * pairs * HD, bytes_accessed=tokens * HD * 12, transcendentals=pairs
        ),
    )(place, seq, rank, parts)


def attention_backward(place, seq, rank, parts, grads, lse, seq_out, cosine, sine, split):
    slots, unused, local_tokens = parts.shape
    tokens = slots * local_tokens
    padded = tokens + TILE
    pairs = tokens * tokens // 2
    return pl.pallas_call(
        functools.partial(backward_kernel, seq.shape[1], slots, local_tokens // BLK, split),
        name="attention_backward",
        out_shape=jax.ShapeDtypeStruct((slots, 3 * HD, local_tokens), bf16),
        grid_spec=pltpu.PrefetchScalarGridSpec(
            num_scalar_prefetch=3,
            grid=(),
            in_specs=whole_vmem(6),
            out_specs=whole_vmem(1)[0],
            scratch_shapes=[
                pltpu.VMEM((HD, padded), bf16),
                pltpu.VMEM((2 * HD, padded), bf16),
                pltpu.VMEM((2 * HD, padded), bf16),
                pltpu.VMEM((padded, 2 * HD), bf16),
                pltpu.VMEM((padded, 2 * HD), bf16),
                pltpu.VMEM((padded, 2 * HD), bf16),
                pltpu.VMEM((8, padded), f32),
                pltpu.VMEM((HD, padded), f32),
                pltpu.VMEM((padded, 2 * HD), f32),
            ],
        ),
        compiler_params=pltpu.CompilerParams(vmem_limit_bytes=62 * 2**20),
        cost_estimate=pl.CostEstimate(
            flops=40 * pairs * HD, bytes_accessed=tokens * HD * 24, transcendentals=pairs
        ),
    )(place, seq, rank, parts, grads, lse, seq_out, cosine, sine)


def swap(value, axis, size, offset):
    return lax.ppermute(value, axis, [(i, i ^ offset) for i in range(size)])


def axis_bits(size):
    return [1 << k for k in range(size.bit_length() - 1)]


def all_sum(value, axis, size):
    for bit in axis_bits(size):
        value = value + swap(value, axis, size, bit)
    return value


def slot_order(bits):
    if not bits:
        return [0]
    rest = slot_order(bits[1:])
    return [s | bits[0] for s in rest] + rest


def product_kernel(dims, tiles, orders, table_ref, *refs):
    step = pl.program_id(0)
    count = len(orders[0])
    pieces = [refs[k * (count + 1) : k * (count + 1) + count] for k in range(len(dims))]
    factors = [refs[k * (count + 1) + count] for k in range(len(dims))]
    refs = refs[len(dims) * (count + 1) :]
    refs, stacks = refs[: -len(dims)], refs[-len(dims) :]

    @pl.when(step == 0)
    def _():
        for stack, parts, (lhs_dim, unused) in zip(stacks, pieces, dims):
            rows = parts[0].shape[1 - lhs_dim]
            for p, part in enumerate(parts):
                if lhs_dim == 0:
                    stack[:, p * rows : (p + 1) * rows] = part[...]
                else:
                    stack[p * rows : (p + 1) * rows, :] = part[...]

    at = 0
    for stack, factor, (lhs_dim, rhs_dim) in zip(stacks, factors, dims):
        product = lax.dot_general(
            stack[...],
            factor[...],
            (((lhs_dim,), (rhs_dim,)), ((), ())),
            preferred_element_type=f32,
        )
        columns = slice(at, at + product.shape[1])
        at += product.shape[1]
        if len(refs) == 1:
            refs[0][:, columns] = product.astype(bf16)
            continue
        added, outs = refs[0], refs[1:]
        product = (product + added[:, columns].astype(f32)).astype(bf16)
        rows = product.shape[0] // count
        for half, order in enumerate(orders):

            @pl.when(step // tiles == half)
            def _(half=half, order=order, product=product, columns=columns, rows=rows):
                for p, slot in enumerate(order):
                    source = orders[0].index(slot)
                    out = outs[2 * half + p // (count // 2)]
                    first = p % (count // 2) * rows
                    out[first : first + rows, columns] = product[
                        source * rows : (source + 1) * rows
                    ]


def piece_products(owners, size, pairs, orders, added):
    count = len(orders[0])
    tiles = 2 if len(pairs) == 1 else 1
    in_specs, operands, scratch, width, flops = [], [], [], 0, 0
    for lhs, rhs, lhs_dim, rhs_dim in pairs:
        tokens = lhs.shape[lhs_dim]
        rows = lhs.shape[1 - lhs_dim] // size
        columns = rhs.shape[1 - rhs_dim] // (2 * tiles)
        width += columns
        flops += 4 * tiles * count * rows * columns * tokens
        for p in range(count):
            if lhs_dim == 0:
                in_specs.append(pl.BlockSpec((tokens, rows), lambda i, t, p=p: (0, t[p])))
            else:
                in_specs.append(pl.BlockSpec((rows, tokens), lambda i, t, p=p: (t[p], 0)))
            operands.append(lhs)
        if rhs_dim == 0:
            in_specs.append(pl.BlockSpec((tokens, columns), lambda i, t: (0, i)))
        else:
            in_specs.append(pl.BlockSpec((columns, tokens), lambda i, t: (i, 0)))
        operands.append(rhs)
        stack = (tokens, count * rows) if lhs_dim == 0 else (count * rows, tokens)
        scratch.append(pltpu.VMEM(stack, bf16))
    if added is None:
        out_shape = [jax.ShapeDtypeStruct((count * rows, 2 * tiles * width), bf16)]
        out_specs = [pl.BlockSpec((count * rows, width), lambda i, t: (0, i))]
    else:
        in_specs.append(pl.BlockSpec((count * rows, width), lambda i, t: (0, i)))
        operands.append(added)
        out_shape = [jax.ShapeDtypeStruct((count // 2 * rows, tiles * width), bf16)] * 4
        out_specs = [
            pl.BlockSpec(
                (count // 2 * rows, width),
                lambda i, t, at=half * tiles: (0, jnp.clip(i - at, 0, tiles - 1)),
            )
            for half in (0, 0, 1, 1)
        ]
    dims = [(lhs_dim, rhs_dim) for unused, unused_too, lhs_dim, rhs_dim in pairs]
    return pl.pallas_call(
        functools.partial(product_kernel, dims, tiles, orders),
        name="piece_products",
        out_shape=out_shape,
        grid_spec=pltpu.PrefetchScalarGridSpec(
            num_scalar_prefetch=1,
            grid=(2 * tiles,),
            in_specs=in_specs,
            out_specs=out_specs,
            scratch_shapes=scratch,
        ),
        compiler_params=pltpu.CompilerParams(vmem_limit_bytes=52 * 2**20),
        cost_estimate=pl.CostEstimate(
            flops=flops,
            bytes_accessed=4 * tiles * width * (2 * count * rows + tokens),
            transcendentals=0,
        ),
    )(owners.astype(jnp.int32), *operands)


def halves_orders(size):
    upper = axis_bits(size)[1:]
    return [(upper, slot_order(upper)), (upper[::-1], slot_order(upper[::-1]))]


def tie(*values):
    return lax.optimization_barrier(values)


class PieceSum:
    def __init__(self, index, size, *pairs):
        self.index, self.size = index, size
        self.orders = halves_orders(size)
        self.bits = [bits for bits, unused in self.orders]
        self.pairs = pairs
        self.spreading = self.finished = False

    def swaps(self, values):
        bits = [half[self.level] for half in self.bits]
        self.pending = [swap(v, "dp", self.size, bit) for v, bit in zip(values, bits)]

    def across_cores(self):
        far = self.index ^ jnp.array([s | 1 for s in self.orders[0][1]], jnp.int32)
        orders = [order for unused, order in self.orders]
        self.kept = piece_products(far, self.size, self.pairs, orders, None)
        self.pending = [swap(self.kept[0], "dp", self.size, 1)]

    def products(self):
        near = self.index ^ jnp.array(self.orders[0][1], jnp.int32)
        orders = [order for unused, order in self.orders]
        made = piece_products(near, self.size, self.pairs, orders, self.pending[0])
        sends, self.kept = [made[0], made[2]], [made[1], made[3]]
        self.level = 0
        self.swaps(sends)

    def advance(self):
        if self.spreading:
            self.advance_spread()
            return
        self.level += 1
        if self.level < len(self.bits[0]):
            sends, keeps = [], []
            for keep, got in zip(self.kept, self.pending):
                cut = keep.shape[0] // 2
                sends.append((keep[:cut].astype(f32) + got[:cut].astype(f32)).astype(bf16))
                keeps.append((keep[cut:].astype(f32) + got[cut:].astype(f32)).astype(bf16))
            self.kept = keeps
            self.swaps(sends)
            return
        self.kept = [
            (keep.astype(f32) + got.astype(f32)).astype(bf16)
            for keep, got in zip(self.kept, self.pending)
        ]
        self.slots = [[0], [0]]
        self.spreading = True
        self.level -= 1
        self.swaps(self.kept)

    def advance_spread(self):
        if self.level > 0:
            self.kept = [jnp.concatenate(p, axis=0) for p in zip(self.kept, self.pending)]
            self.slots = [
                have + [s | half[self.level] for s in have]
                for have, half in zip(self.slots, self.bits)
            ]
            self.level -= 1
            self.swaps(self.kept)
            if self.level == 0:
                self.early = [swap(v, "dp", self.size, 1) for v in self.kept]
        elif self.level == 0:
            self.others = self.pending
            self.level = -1
            self.pending = [swap(v, "dp", self.size, 1) for v in self.others]
        else:
            self.finished = True

    def complete(self, level):
        while not self.spreading or self.level > level:
            arrived([self])
            self.advance()

    def spread_first(self, *layout):
        self.complete(0)
        self.layout = layout
        slots = [s | core for have in self.slots for core in (0, 1) for s in have]
        arrays = [v for pair in zip(self.kept, self.early) for v in pair]
        self.outs = spread(self.index, self.size, arrays, slots, layout, None)

    def spread_second(self):
        self.complete(-1)
        slots = [
            s | bits[0] | core
            for have, bits in zip(self.slots, self.bits)
            for core in (0, 1)
            for s in have
        ]
        arrays = [v for pair in zip(self.others, self.pending) for v in pair]
        return spread(self.index, self.size, arrays, slots, self.layout, self.outs)


def arrived(sums, *values):
    count = [len(s.pending) for s in sums]
    out = list(tie(*[p for s in sums for p in s.pending], *values))
    for s, n in zip(sums, count):
        s.pending, out = out[:n], out[n:]
    return out


def computed(sums, *values):
    count = [len(s.kept) for s in sums]
    out = list(tie(*[p for s in sums for p in s.kept], *values))
    for s, n in zip(sums, count):
        s.kept, out = out[:n], out[n:]
    return out


def spread_kernel(quarter, layout, table_ref, *refs):
    ins, outs = refs[:4], refs[-len(layout) :]
    step = pl.program_id(0)
    for j, piece in enumerate(ins):

        @pl.when(step // quarter == j)
        def _(piece=piece):
            at = 0
            for out, (parts, columns, transposed) in zip(outs, layout):
                for c in range(parts):
                    block = piece[:, at : at + columns].astype(f32)
                    at += columns
                    if parts > 1:
                        out[c] = block
                    else:
                        out[...] = jnp.transpose(block) if transposed else block


def spread(index, size, arrays, slots, layout, into):
    table = index ^ jnp.array(slots, jnp.int32)
    quarter, half = size // 4, size // 2
    rows, width = arrays[0].shape[0] // quarter, arrays[0].shape[1]
    in_specs = [
        pl.BlockSpec(
            (rows, width),
            lambda i, t, at=j * quarter: (jnp.clip(i - at, 0, quarter - 1), 0),
        )
        for j in range(4)
    ]
    out_shape, out_specs = [], []
    for parts, columns, transposed in layout:
        if parts > 1:
            out_shape.append((parts, rows * size, 2 * columns))
            out_specs.append(
                pl.BlockSpec((parts, rows, columns), lambda i, t: (0, t[i], i // half))
            )
        elif transposed:
            out_shape.append((2 * columns, rows * size))
            out_specs.append(pl.BlockSpec((columns, rows), lambda i, t: (i // half, t[i])))
        else:
            out_shape.append((rows * size, 2 * columns))
            out_specs.append(pl.BlockSpec((rows, columns), lambda i, t: (t[i], i // half)))
    aliases = {}
    if into is not None:
        aliases = {1 + len(arrays) + k: k for k in range(len(layout))}
        in_specs += [pl.BlockSpec(memory_space=pl.ANY)] * len(layout)
        arrays = arrays + list(into)
    return pl.pallas_call(
        functools.partial(spread_kernel, quarter, layout),
        input_output_aliases=aliases,
        name="spread",
        out_shape=[jax.ShapeDtypeStruct(shape, f32) for shape in out_shape],
        grid_spec=pltpu.PrefetchScalarGridSpec(
            num_scalar_prefetch=1, grid=(size,), in_specs=in_specs, out_specs=out_specs
        ),
        compiler_params=pltpu.CompilerParams(vmem_limit_bytes=48 * 2**20),
        cost_estimate=pl.CostEstimate(
            flops=0, bytes_accessed=rows * width * size * 6, transcendentals=0
        ),
    )(table, *arrays)


def local(
    dp_size,
    hidden_in,
    gain,
    bias,
    w_qkv,
    b_qkv,
    w_dense,
    b_dense,
    w_fc1,
    b_fc1,
    w_fc2,
    b_fc2,
    cotangent,
    seq_lengths,
    padding,
    block_perm,
):
    tok_local, dim_local = hidden_in.shape
    model_width = gain.shape[0]
    heads = w_qkv.shape[2] // HD
    split = dp_size // heads
    subs = tok_local // BLK
    nblk = block_perm.shape[0]
    data_index = lax.axis_index("dp")
    tensor_index = lax.axis_index("tensor")
    pos_all, valid_all = token_table(seq_lengths, padding, block_perm)
    my_pos = lax.dynamic_slice_in_dim(pos_all, data_index * tok_local, tok_local)
    my_valid = lax.dynamic_slice_in_dim(valid_all, data_index * tok_local, tok_local)
    cosine, sine = rotary_tables(my_pos)
    cosine_all, sine_all = rotary_tables(jnp.arange(nblk * BLK, dtype=jnp.int32))
    place = jnp.concatenate([block_perm, pos_all[::BLK] // BLK])
    seq = jnp.stack([jnp.cumsum(seq_lengths) - seq_lengths, seq_lengths])
    rank = (data_index // heads).reshape(1).astype(jnp.int32)

    def to_heads(stacked):
        stacked = jnp.concatenate([stacked] * split) if split > 1 else stacked
        return lax.all_to_all(stacked, "dp", 0, 0, tiled=True)

    def to_tokens(stacked):
        got = lax.all_to_all(stacked, "dp", 0, 0, tiled=True)
        if split > 1:
            got = got.reshape(split, heads, *got.shape[1:]).astype(f32)
            got = jnp.sum(got, axis=0).astype(bf16)
        return got

    full_in = lax.all_gather(hidden_in.astype(bf16), "tensor", axis=1, tiled=True)
    grad_proj = lax.all_gather(cotangent.astype(bf16), "tensor", axis=1, tiled=True)
    w_back = row_major(jnp.transpose(w_qkv, (1, 2, 0)))
    full_in, w_back, cosine, sine, cosine_all, sine_all, place, seq = tie(
        full_in, w_back, cosine, sine, cosine_all, sine_all, place, seq
    )
    full_in = full_in.astype(f32)
    row_mean = jnp.mean(full_in, axis=-1, keepdims=True)
    centered = full_in - row_mean
    inv_std = lax.rsqrt(jnp.mean(centered * centered, axis=-1, keepdims=True) + epsilon)
    normal_x = centered * inv_std
    normed = (normal_x * gain + bias).astype(bf16)
    projections = (
        jnp.einsum("td,dcf->cft", normed, w_qkv, preferred_element_type=f32) + b_qkv[:, :, None]
    ).reshape(3, heads, HD, tok_local)
    turned = projections[:2, :, :ROT].reshape(2, heads, 2, HALF, tok_local)
    lower, upper = turned[:, :, 0], turned[:, :, 1]
    rotated = jnp.concatenate(
        [
            lower * cosine - upper * sine,
            upper * cosine + lower * sine,
            projections[:2, :, ROT:],
        ],
        axis=2,
    )
    packed = jnp.concatenate([rotated[0], rotated[1], projections[2]], axis=1).astype(bf16)
    parts = to_heads(packed)
    hidden_pre = jnp.dot(normed, w_fc1, preferred_element_type=f32) + b_fc1
    activated = gelu_tanh(hidden_pre).astype(bf16)
    activated_t, normed_t = row_major(jnp.transpose(activated)), row_major(jnp.transpose(normed))
    parts, hidden_pre, activated, activated_t, normed_t, grad_proj = tie(
        parts, hidden_pre, activated, activated_t, normed_t, grad_proj
    )

    def new_sum(*pairs):
        made = PieceSum(data_index, dp_size, *pairs)
        made.across_cores()
        return made

    sum_fc2 = new_sum((activated_t, grad_proj, 1, 0))
    (grad_proj,) = computed([sum_fc2], grad_proj)
    grad_attended = jnp.einsum(
        "ed,td->et", w_dense, grad_proj, preferred_element_type=f32
    ).astype(bf16)
    (grad_attended,) = arrived([sum_fc2], grad_attended)
    grad_stack = to_heads(grad_attended.reshape(heads, HD, tok_local))
    sum_fc2.products()
    grad_proj, hidden_pre = computed([sum_fc2], grad_proj, hidden_pre)
    grad_act = jnp.einsum("td,fd->tf", grad_proj, w_fc2, preferred_element_type=f32)
    unused_value, gelu_back = jax.vjp(gelu_tanh, hidden_pre)
    grad_hidden = gelu_back(grad_act)[0].astype(bf16)
    (grad_hidden,) = arrived([sum_fc2], grad_hidden)
    sum_fc1 = new_sum((normed_t, grad_hidden, 1, 0))
    sum_fc1.kept = arrived([sum_fc1], *sum_fc1.kept)
    sum_fc2.advance()
    sum_fc1.pending = computed([sum_fc2], *sum_fc1.pending)
    sum_fc1.products()
    sum_fc1.kept = arrived([sum_fc2], *sum_fc1.kept)
    sum_fc2.advance()

    (parts,) = computed([sum_fc2, sum_fc1], parts)
    out_stack, lse, seq_out = attention_forward(place, seq, rank, parts, split)
    out_stack, grad_stack, lse = arrived([sum_fc2, sum_fc1], out_stack, grad_stack, lse)
    attended = to_tokens(out_stack).reshape(heads * HD, tok_local)
    sum_fc2.advance()
    sum_fc1.advance()
    (lse,) = computed([sum_fc2, sum_fc1], lse)
    grad_pieces = attention_backward(
        place, seq, rank, parts, grad_stack, lse, seq_out, cosine_all, sine_all, split
    )
    grad_pieces, attended, grad_hidden, activated = arrived(
        [sum_fc2, sum_fc1], grad_pieces, attended, grad_hidden, activated
    )

    grad_qkv = to_tokens(grad_pieces).reshape(heads, 3, HD, tok_local)
    partial_value = jnp.einsum(
        "et,ed->td", attended, w_dense, preferred_element_type=f32
    ) + jnp.dot(activated, w_fc2, preferred_element_type=f32)
    partial_value = partial_value.astype(bf16)
    projected = lax.psum_scatter(
        partial_value, "tensor", scatter_dimension=1, tiled=True
    ).astype(f32)
    arrived([sum_fc2, sum_fc1], partial_value)
    sum_fc1.advance()
    sum_fc2.advance()
    (grad_hidden,) = computed([sum_fc1], grad_hidden)
    grad_normed = jnp.einsum("tf,df->td", grad_hidden, w_fc1, preferred_element_type=f32)
    (grad_normed,) = arrived([sum_fc1], grad_normed)
    sum_fc1.advance()
    grad_qkv, grad_normed, *sum_fc1.kept = tie(grad_qkv, grad_normed, *sum_fc1.kept)
    branch = projected + b_dense + b_fc2
    output = hidden_in + branch
    valid_rows = my_valid.astype(f32)[:, None]
    sum_output = jnp.sum(output * output * valid_rows)
    sum_branch = jnp.sum(branch * branch * valid_rows)
    valid_count = jnp.sum(valid_all.astype(f32)) * model_width

    grad_b_fc1 = jnp.sum(grad_hidden.astype(f32), axis=0)
    grad_b_qkv = jnp.transpose(jnp.sum(grad_qkv.astype(f32), axis=3), (1, 0, 2))
    by_half = jnp.transpose(
        grad_qkv.reshape(2, heads // 2, 3, HD, tok_local), (0, 2, 1, 3, 4)
    ).reshape(3 * heads * HD, tok_local)
    sum_qkv = new_sum((normed_t, by_half, 1, 1), (grad_proj, attended, 0, 1))
    (grad_qkv,) = computed([sum_qkv], grad_qkv)
    grad_normed = row_major(
        grad_normed
        + jnp.einsum(
            "hcet,ched->td",
            grad_qkv,
            w_back.reshape(3, heads, HD, model_width),
            preferred_element_type=f32,
        )
    )
    grad_narrow = grad_normed.astype(bf16)
    (grad_narrow,) = arrived([sum_qkv, sum_fc1], grad_narrow)
    grad_local = lax.psum_scatter(
        grad_narrow, "tensor", scatter_dimension=1, tiled=True
    ).astype(f32)
    sum_qkv.products()
    sum_fc1.advance()
    sum_fc2.kept = computed([sum_qkv], *sum_fc2.kept)
    sum_fc2.spread_first((1, model_width // 2, False))
    sum_fc2.outs = arrived([sum_qkv], *sum_fc2.outs)
    sum_qkv.advance()
    sum_fc2.pending = computed([sum_qkv], *sum_fc2.pending)
    (grad_w_fc2,) = sum_fc2.spread_second()
    (grad_w_fc2,) = arrived([sum_qkv], grad_w_fc2)
    sum_qkv.advance()
    scaled = grad_normed * gain
    mean_sums = jnp.stack([jnp.sum(scaled, axis=1), jnp.sum(scaled * normal_x, axis=1)])
    shared = jnp.concatenate([mean_sums.reshape(-1), sum_output[None], sum_branch[None]])
    sum_fc1.complete(0)
    sum_fc1.early = computed([sum_qkv], *sum_fc1.early)
    sum_fc1.spread_first((1, w_fc1.shape[1] // 2, False))
    sum_fc1.outs = arrived([sum_qkv], *sum_fc1.outs)
    sum_qkv.advance()
    sum_fc1.pending = computed([sum_qkv], *sum_fc1.pending)
    (grad_w_fc1,) = sum_fc1.spread_second()
    shared = all_sum(shared, "tensor", model_width // dim_local)
    mean_sums = shared[:-2].reshape(2, tok_local) / model_width
    mean_one, mean_two = mean_sums[0][:, None], mean_sums[1][:, None]
    gain_local = lax.dynamic_slice_in_dim(gain, tensor_index * dim_local, dim_local)
    normal_local = lax.dynamic_slice_in_dim(normal_x, tensor_index * dim_local, dim_local, 1)
    grad_input = cotangent + inv_std * (
        grad_local * gain_local - mean_one - normal_local * mean_two
    )
    late = jnp.concatenate(
        [
            jnp.sum(grad_local * normal_local, axis=0),
            jnp.sum(grad_local, axis=0),
            jnp.sum(cotangent, axis=0),
            grad_b_fc1,
            grad_b_qkv.reshape(-1),
            shared[-2:],
        ]
    )
    cuts = [dim_local, 2 * dim_local, 3 * dim_local, 3 * dim_local + grad_b_fc1.shape[0]]
    late = all_sum(late, "dp", dp_size)
    sum_qkv.complete(0)
    sum_qkv.early[0], grad_w_fc1 = tie(sum_qkv.early[0], grad_w_fc1)
    sum_qkv.spread_first((3, heads * HD // 2, False), (1, heads * HD // 2, True))
    sum_qkv.outs = arrived([sum_qkv], *sum_qkv.outs)
    sum_qkv.advance()
    sum_qkv.complete(-1)
    sum_qkv.pending[0], late = tie(sum_qkv.pending[0], late)
    grad_w_qkv, grad_w_dense = sum_qkv.spread_second()
    grad_w_qkv = jnp.transpose(grad_w_qkv, (1, 0, 2))
    totals = late[-2:]
    rms = jnp.sqrt(totals / valid_count)
    bias_grad = late[cuts[1] : cuts[2]]
    return (
        output,
        grad_input,
        late[: cuts[0]],
        late[cuts[0] : cuts[1]],
        grad_w_qkv,
        late[cuts[3] : -2].reshape(3, heads * HD),
        grad_w_dense,
        bias_grad,
        grad_w_fc1,
        late[cuts[2] : cuts[3]],
        grad_w_fc2,
        bias_grad,
        rms[0],
        rms[1],
    )


def solution(mesh):
    return jax.shard_map(
        functools.partial(local, mesh.shape["dp"]),
        mesh=mesh,
        in_specs=(
            P("dp", "tensor"),
            P(),
            P(),
            P(None, None, "tensor"),
            P(None, "tensor"),
            P("tensor", None),
            P("tensor"),
            P(None, "tensor"),
            P("tensor"),
            P("tensor", None),
            P("tensor"),
            P("dp", "tensor"),
            P(),
            P(),
            P(),
        ),
        out_specs=(
            P("dp", "tensor"),
            P("dp", "tensor"),
            P("tensor"),
            P("tensor"),
            P(None, None, "tensor"),
            P(None, "tensor"),
            P("tensor", None),
            P("tensor"),
            P(None, "tensor"),
            P("tensor"),
            P("tensor", None),
            P("tensor"),
            P(),
            P(),
        ),
        check_vma=False,
    )
```

```python
import functools

import jax
import jax.numpy as jnp
from jax import lax
from jax.experimental import pallas as pl
from jax.experimental.layout import Layout, with_layout_constraint
from jax.experimental.pallas import tpu as pltpu
from jax.sharding import PartitionSpec as P

HD = 64
ROT = 32
HALF = ROT // 2
BLK = 128
TILE = 512

epsilon = 1e-05
masked_score = -1e30
far_score = 1e30
log2e = 1.4426950408889634
f32 = jnp.float32
bf16 = jnp.bfloat16


def row_major(value):
    return with_layout_constraint(value, Layout(tuple(range(value.ndim))))


def token_table(seq_lengths, padding, initial):
    seq_count = seq_lengths.shape[0]
    seq_ends = jnp.cumsum(seq_lengths)
    seq_starts = seq_ends - seq_lengths
    seq_block = jnp.sum((initial[:, None] >= seq_ends[None, :]).astype(jnp.int32), axis=1)
    members = (seq_block[:, None] == jnp.arange(seq_count, dtype=jnp.int32)[None, :]).astype(
        jnp.int32
    )
    first_block = jnp.sum(members * seq_starts[None, :], axis=1)
    limits = jnp.sum(members * (seq_lengths * BLK - padding)[None, :], axis=1)
    offsets = jnp.arange(BLK, dtype=jnp.int32)
    positions = (initial - first_block)[:, None] * BLK + offsets[None, :]
    is_valid = positions < limits[:, None]
    return (positions.reshape(-1), is_valid.reshape(-1))


def rotary_tables(positions):
    frequency = 10000.0 ** (-jnp.arange(0, ROT, 2, dtype=f32) / ROT)
    angles = frequency[:, None] * positions.astype(f32)[None, :]
    return (jnp.cos(angles), jnp.sin(angles))


def gelu_tanh(gelu_input):
    return jax.nn.gelu(gelu_input, approximate=True)


def dot_f32(a, b):
    return lax.dot_general(a, b, (((1,), (0,)), ((), ())), preferred_element_type=f32)


def flip(block):
    return jnp.transpose(block.astype(f32)).astype(bf16)


def each_query_tile(seq_ref, rank_ref, seq_count, split, body):
    def one_seq(s, count):
        start = seq_ref[0, s] * BLK
        length = seq_ref[1, s] * BLK
        tiles = (length + TILE - 1) // TILE

        def one_tile(i, unused):
            if split == 1:
                body(start, length, i, tiles)
            else:

                @pl.when(lax.rem(count + i, split) == rank_ref[0])
                def _():
                    body(start, length, i, tiles)

            return unused

        lax.fori_loop(0, tiles, one_tile, 0)
        return count + tiles

    lax.fori_loop(0, seq_count, one_seq, 0)


def forward_kernel(seq_count, slots, subs, split, place_ref, seq_ref, rank_ref, *refs):
    parts, outs, lse_ref, seq_out_ref, q_t, keys, v_t = refs
    tokens = slots * subs * BLK
    tail = q_t.shape[1] - tokens
    q_t[:, pl.ds(tokens, tail)] = jnp.zeros((HD, tail), bf16)
    v_t[:, pl.ds(tokens, tail)] = jnp.zeros((HD, tail), bf16)
    keys[pl.ds(tokens, tail), :] = jnp.zeros((tail, HD), bf16)
    if split > 1:
        lse_ref[...] = jnp.zeros(lse_ref.shape, f32)
        seq_out_ref[...] = jnp.zeros(seq_out_ref.shape, bf16)
    @pl.loop(0, slots)
    def _(s):
        for b in range(subs):
            where = pl.multiple_of(place_ref[s * subs + b] * BLK, BLK)
            cols = slice(b * BLK, (b + 1) * BLK)
            q_t[:, pl.ds(where, BLK)] = parts[s, 0:HD, cols]
            keys[pl.ds(where, BLK), :] = flip(parts[s, HD : 2 * HD, cols])
            v_t[:, pl.ds(where, BLK)] = parts[s, 2 * HD :, cols]
    scale = HD ** (-0.5) * log2e
    row = lax.broadcasted_iota(jnp.int32, (TILE, TILE), 0)
    col = lax.broadcasted_iota(jnp.int32, (TILE, TILE), 1)

    def tile(start, length, i, tiles):
        q_at = pl.multiple_of(start + i * TILE, BLK)
        q_tile = q_t[:, pl.ds(q_at, TILE)]

        def step(j, carried, diagonal):
            run_max, run_sum, acc = carried
            k_at = pl.multiple_of(start + j * TILE, BLK)
            scores = dot_f32(keys[pl.ds(k_at, TILE), :], q_tile) * scale
            if diagonal:
                scores = jnp.where(row <= col, scores, masked_score)
            new_max = jnp.maximum(run_max, jnp.max(scores, axis=0, keepdims=True))
            factor = jnp.exp2(run_max - new_max)
            weights = jnp.exp2(scores - new_max)
            run_sum = run_sum * factor + jnp.sum(weights, axis=0, keepdims=True)
            acc = acc * factor + dot_f32(v_t[:, pl.ds(k_at, TILE)], weights.astype(bf16))
            return new_max, run_sum, acc

        carried = (
            jnp.full((1, TILE), masked_score, f32),
            jnp.zeros((1, TILE), f32),
            jnp.zeros((HD, TILE), f32),
        )
        carried = lax.fori_loop(0, i, lambda j, c: step(j, c, False), carried)
        run_max, run_sum, acc = step(i, carried, True)
        lse_ref[:, pl.ds(q_at, TILE)] = jnp.broadcast_to(run_max + jnp.log2(run_sum), (8, TILE))
        seq_out_ref[:, pl.ds(q_at, TILE)] = (acc / run_sum).astype(bf16)

    each_query_tile(seq_ref, rank_ref, seq_count, split, tile)
    @pl.loop(0, slots)
    def _(s):
        for b in range(subs):
            where = pl.multiple_of(place_ref[s * subs + b] * BLK, BLK)
            outs[s, :, b * BLK : (b + 1) * BLK] = seq_out_ref[:, pl.ds(where, BLK)]


def backward_kernel(seq_count, slots, subs, split, place_ref, seq_ref, rank_ref, *refs):
    parts, grads, lse_ref, seq_out_ref, cos_ref, sin_ref, outs = refs[:7]
    k_t, q_up, g_down, kv, q_left, g_right, row_dot, dq_t, dkv = refs[7:]
    tokens = slots * subs * BLK
    tail = k_t.shape[1] - tokens
    q_up[HD:, :] = jnp.zeros((HD, tokens + tail), bf16)
    g_down[:HD, :] = jnp.zeros((HD, tokens + tail), bf16)
    k_t[:, pl.ds(tokens, tail)] = jnp.zeros((HD, tail), bf16)
    q_up[:HD, pl.ds(tokens, tail)] = jnp.zeros((HD, tail), bf16)
    g_down[HD:, pl.ds(tokens, tail)] = jnp.zeros((HD, tail), bf16)
    row_dot[:, pl.ds(tokens, tail)] = jnp.zeros((8, tail), f32)
    for wide in (kv, q_left, g_right):
        wide[pl.ds(tokens, tail), :] = jnp.zeros((tail, 2 * HD), bf16)
    dq_t[...] = jnp.zeros(dq_t.shape, f32)
    dkv[...] = jnp.zeros(dkv.shape, f32)
    left = lax.broadcasted_iota(jnp.int32, (BLK, 2 * HD), 1) < HD
    @pl.loop(0, slots)
    def _(s):
        for b in range(subs):
            where = pl.multiple_of(place_ref[s * subs + b] * BLK, BLK)
            cols = slice(b * BLK, (b + 1) * BLK)
            at = pl.ds(where, BLK)
            q_blk = parts[s, 0:HD, cols]
            g_blk = grads[s, :, cols]
            q_up[:HD, at] = q_blk
            g_down[HD:, at] = g_blk
            k_t[:, at] = parts[s, HD : 2 * HD, cols]
            kv[at, :] = flip(parts[s, HD:, cols])
            both = jnp.transpose(jnp.concatenate([q_blk.astype(f32), g_blk.astype(f32)], axis=0))
            q_left[at, :] = jnp.where(left, both, 0.0).astype(bf16)
            g_right[at, :] = jnp.where(left, 0.0, both).astype(bf16)
            dots = jnp.sum(
                g_blk.astype(f32) * seq_out_ref[:, at].astype(f32), axis=0, keepdims=True
            )
            row_dot[:, at] = jnp.broadcast_to(dots, (8, BLK))
    scale = HD ** (-0.5)
    row = lax.broadcasted_iota(jnp.int32, (TILE, TILE), 0)
    col = lax.broadcasted_iota(jnp.int32, (TILE, TILE), 1)
    lane = lax.broadcasted_iota(jnp.int32, (1, TILE), 1)

    def pair(start, length, i, j, diagonal):
        q_at = pl.ds(pl.multiple_of(start + i * TILE, BLK), TILE)
        k_at = pl.ds(pl.multiple_of(start + j * TILE, BLK), TILE)
        lse = jnp.where(i * TILE + lane < length, lse_ref[0:1, q_at], far_score)
        kv_tile = kv[k_at, :]
        scores = dot_f32(kv_tile, q_up[:, q_at]) * (scale * log2e)
        if diagonal:
            scores = jnp.where(row <= col, scores, masked_score)
        probs = jnp.exp2(scores - lse)
        grad_probs = dot_f32(kv_tile, g_down[:, q_at])
        grad_scores = (probs * (grad_probs - row_dot[0:1, q_at])).astype(bf16)
        probs = probs.astype(bf16)
        dkv[k_at, :] += dot_f32(grad_scores, q_left[q_at, :]) + dot_f32(probs, g_right[q_at, :])
        return dot_f32(k_t[:, k_at], grad_scores)

    def tile(start, length, i, tiles):
        total = pair(start, length, i, i, True)
        total = lax.fori_loop(
            0, i, lambda j, c: c + pair(start, length, i, j, False), total
        )
        dq_t[:, pl.ds(pl.multiple_of(start + i * TILE, BLK), TILE)] = total

    each_query_tile(seq_ref, rank_ref, seq_count, split, tile)

    def unrotate(head_block, cosine, sine):
        lower = head_block[:HALF]
        upper = head_block[HALF:ROT]
        return jnp.concatenate(
            [
                lower * cosine + upper * sine,
                upper * cosine - lower * sine,
                head_block[ROT:],
            ],
            axis=0,
        )

    @pl.loop(0, slots)
    def _(s):
        for b in range(subs):
            where = pl.multiple_of(place_ref[s * subs + b] * BLK, BLK)
            at = pl.ds(where, BLK)
            first = pl.multiple_of(place_ref[slots * subs + s * subs + b] * BLK, BLK)
            cosine = cos_ref[:, pl.ds(first, BLK)]
            sine = sin_ref[:, pl.ds(first, BLK)]
            cols = slice(b * BLK, (b + 1) * BLK)
            outs[s, 0:HD, cols] = unrotate(dq_t[:, at] * scale, cosine, sine).astype(bf16)
            pair_t = jnp.transpose(dkv[at, :])
            outs[s, HD : 2 * HD, cols] = unrotate(pair_t[:HD] * scale, cosine, sine).astype(bf16)
            outs[s, 2 * HD :, cols] = pair_t[HD:].astype(bf16)


def whole_vmem(count):
    return [pl.BlockSpec(memory_space=pltpu.VMEM)] * count


def attention_forward(place, seq, rank, parts, split):
    slots, unused, local_tokens = parts.shape
    tokens = slots * local_tokens
    padded = tokens + TILE
    pairs = tokens * tokens // 2
    return pl.pallas_call(
        functools.partial(forward_kernel, seq.shape[1], slots, local_tokens // BLK, split),
        name="attention_forward",
        out_shape=[
            jax.ShapeDtypeStruct((slots, HD, local_tokens), bf16),
            jax.ShapeDtypeStruct((8, padded), f32),
            jax.ShapeDtypeStruct((HD, padded), bf16),
        ],
        grid_spec=pltpu.PrefetchScalarGridSpec(
            num_scalar_prefetch=3,
            grid=(),
            in_specs=whole_vmem(1),
            out_specs=whole_vmem(3),
            scratch_shapes=[
                pltpu.VMEM((HD, padded), bf16),
                pltpu.VMEM((padded, HD), bf16),
                pltpu.VMEM((HD, padded), bf16),
            ],
        ),
        compiler_params=pltpu.CompilerParams(vmem_limit_bytes=60 * 2**20),
        cost_estimate=pl.CostEstimate(
            flops=16 * pairs * HD, bytes_accessed=tokens * HD * 12, transcendentals=pairs
        ),
    )(place, seq, rank, parts)


def attention_backward(place, seq, rank, parts, grads, lse, seq_out, cosine, sine, split):
    slots, unused, local_tokens = parts.shape
    tokens = slots * local_tokens
    padded = tokens + TILE
    pairs = tokens * tokens // 2
    return pl.pallas_call(
        functools.partial(backward_kernel, seq.shape[1], slots, local_tokens // BLK, split),
        name="attention_backward",
        out_shape=jax.ShapeDtypeStruct((slots, 3 * HD, local_tokens), bf16),
        grid_spec=pltpu.PrefetchScalarGridSpec(
            num_scalar_prefetch=3,
            grid=(),
            in_specs=whole_vmem(6),
            out_specs=whole_vmem(1)[0],
            scratch_shapes=[
                pltpu.VMEM((HD, padded), bf16),
                pltpu.VMEM((2 * HD, padded), bf16),
                pltpu.VMEM((2 * HD, padded), bf16),
                pltpu.VMEM((padded, 2 * HD), bf16),
                pltpu.VMEM((padded, 2 * HD), bf16),
                pltpu.VMEM((padded, 2 * HD), bf16),
                pltpu.VMEM((8, padded), f32),
                pltpu.VMEM((HD, padded), f32),
                pltpu.VMEM((padded, 2 * HD), f32),
            ],
        ),
        compiler_params=pltpu.CompilerParams(vmem_limit_bytes=62 * 2**20),
        cost_estimate=pl.CostEstimate(
            flops=40 * pairs * HD, bytes_accessed=tokens * HD * 24, transcendentals=pairs
        ),
    )(place, seq, rank, parts, grads, lse, seq_out, cosine, sine)


def swap(value, axis, size, offset):
    return lax.ppermute(value, axis, [(i, i ^ offset) for i in range(size)])


def axis_bits(size):
    return [1 << k for k in range(size.bit_length() - 1)]


def all_sum(value, axis, size):
    for bit in axis_bits(size):
        value = value + swap(value, axis, size, bit)
    return value


def slot_order(bits):
    if not bits:
        return [0]
    rest = slot_order(bits[1:])
    return [s | bits[0] for s in rest] + rest


def product_kernel(dims, tiles, orders, table_ref, *refs):
    step = pl.program_id(0)
    count = len(orders[0])
    pieces = [refs[k * (count + 1) : k * (count + 1) + count] for k in range(len(dims))]
    factors = [refs[k * (count + 1) + count] for k in range(len(dims))]
    refs = refs[len(dims) * (count + 1) :]
    refs, stacks = refs[: -len(dims)], refs[-len(dims) :]

    @pl.when(step == 0)
    def _():
        for stack, parts, (lhs_dim, unused) in zip(stacks, pieces, dims):
            rows = parts[0].shape[1 - lhs_dim]
            for p, part in enumerate(parts):
                if lhs_dim == 0:
                    stack[:, p * rows : (p + 1) * rows] = part[...]
                else:
                    stack[p * rows : (p + 1) * rows, :] = part[...]

    at = 0
    for stack, factor, (lhs_dim, rhs_dim) in zip(stacks, factors, dims):
        product = lax.dot_general(
            stack[...],
            factor[...],
            (((lhs_dim,), (rhs_dim,)), ((), ())),
            preferred_element_type=f32,
        )
        columns = slice(at, at + product.shape[1])
        at += product.shape[1]
        if len(refs) == 1:
            refs[0][:, columns] = product.astype(bf16)
            continue
        added, outs = refs[0], refs[1:]
        product = (product + added[:, columns].astype(f32)).astype(bf16)
        rows = product.shape[0] // count
        for half, order in enumerate(orders):

            @pl.when(step // tiles == half)
            def _(half=half, order=order, product=product, columns=columns, rows=rows):
                for p, slot in enumerate(order):
                    source = orders[0].index(slot)
                    out = outs[2 * half + p // (count // 2)]
                    first = p % (count // 2) * rows
                    out[first : first + rows, columns] = product[
                        source * rows : (source + 1) * rows
                    ]


def piece_products(owners, size, pairs, orders, added):
    count = len(orders[0])
    tiles = 2 if len(pairs) == 1 else 1
    in_specs, operands, scratch, width, flops = [], [], [], 0, 0
    for lhs, rhs, lhs_dim, rhs_dim in pairs:
        tokens = lhs.shape[lhs_dim]
        rows = lhs.shape[1 - lhs_dim] // size
        columns = rhs.shape[1 - rhs_dim] // (2 * tiles)
        width += columns
        flops += 4 * tiles * count * rows * columns * tokens
        for p in range(count):
            if lhs_dim == 0:
                in_specs.append(pl.BlockSpec((tokens, rows), lambda i, t, p=p: (0, t[p])))
            else:
                in_specs.append(pl.BlockSpec((rows, tokens), lambda i, t, p=p: (t[p], 0)))
            operands.append(lhs)
        if rhs_dim == 0:
            in_specs.append(pl.BlockSpec((tokens, columns), lambda i, t: (0, i)))
        else:
            in_specs.append(pl.BlockSpec((columns, tokens), lambda i, t: (i, 0)))
        operands.append(rhs)
        stack = (tokens, count * rows) if lhs_dim == 0 else (count * rows, tokens)
        scratch.append(pltpu.VMEM(stack, bf16))
    if added is None:
        out_shape = [jax.ShapeDtypeStruct((count * rows, 2 * tiles * width), bf16)]
        out_specs = [pl.BlockSpec((count * rows, width), lambda i, t: (0, i))]
    else:
        in_specs.append(pl.BlockSpec((count * rows, width), lambda i, t: (0, i)))
        operands.append(added)
        out_shape = [jax.ShapeDtypeStruct((count // 2 * rows, tiles * width), bf16)] * 4
        out_specs = [
            pl.BlockSpec(
                (count // 2 * rows, width),
                lambda i, t, at=half * tiles: (0, jnp.clip(i - at, 0, tiles - 1)),
            )
            for half in (0, 0, 1, 1)
        ]
    dims = [(lhs_dim, rhs_dim) for unused, unused_too, lhs_dim, rhs_dim in pairs]
    return pl.pallas_call(
        functools.partial(product_kernel, dims, tiles, orders),
        name="piece_products",
        out_shape=out_shape,
        grid_spec=pltpu.PrefetchScalarGridSpec(
            num_scalar_prefetch=1,
            grid=(2 * tiles,),
            in_specs=in_specs,
            out_specs=out_specs,
            scratch_shapes=scratch,
        ),
        compiler_params=pltpu.CompilerParams(vmem_limit_bytes=52 * 2**20),
        cost_estimate=pl.CostEstimate(
            flops=flops,
            bytes_accessed=4 * tiles * width * (2 * count * rows + tokens),
            transcendentals=0,
        ),
    )(owners.astype(jnp.int32), *operands)


def halves_orders(size):
    upper = axis_bits(size)[1:]
    return [(upper, slot_order(upper)), (upper[::-1], slot_order(upper[::-1]))]


def tie(*values):
    return lax.optimization_barrier(values)


class PieceSum:
    def __init__(self, index, size, *pairs):
        self.index, self.size = index, size
        self.orders = halves_orders(size)
        self.bits = [bits for bits, unused in self.orders]
        self.pairs = pairs
        self.spreading = self.finished = False

    def swaps(self, values):
        bits = [half[self.level] for half in self.bits]
        self.pending = [swap(v, "dp", self.size, bit) for v, bit in zip(values, bits)]

    def across_cores(self):
        far = self.index ^ jnp.array([s | 1 for s in self.orders[0][1]], jnp.int32)
        orders = [order for unused, order in self.orders]
        self.kept = piece_products(far, self.size, self.pairs, orders, None)
        self.pending = [swap(self.kept[0], "dp", self.size, 1)]

    def products(self):
        near = self.index ^ jnp.array(self.orders[0][1], jnp.int32)
        orders = [order for unused, order in self.orders]
        made = piece_products(near, self.size, self.pairs, orders, self.pending[0])
        sends, self.kept = [made[0], made[2]], [made[1], made[3]]
        self.level = 0
        self.swaps(sends)

    def advance(self):
        if self.spreading:
            self.advance_spread()
            return
        self.level += 1
        if self.level < len(self.bits[0]):
            sends, keeps = [], []
            for keep, got in zip(self.kept, self.pending):
                cut = keep.shape[0] // 2
                sends.append((keep[:cut].astype(f32) + got[:cut].astype(f32)).astype(bf16))
                keeps.append((keep[cut:].astype(f32) + got[cut:].astype(f32)).astype(bf16))
            self.kept = keeps
            self.swaps(sends)
            return
        self.kept = [
            (keep.astype(f32) + got.astype(f32)).astype(bf16)
            for keep, got in zip(self.kept, self.pending)
        ]
        self.slots = [[0], [0]]
        self.spreading = True
        self.level -= 1
        self.swaps(self.kept)

    def advance_spread(self):
        if self.level > 0:
            self.kept = [jnp.concatenate(p, axis=0) for p in zip(self.kept, self.pending)]
            self.slots = [
                have + [s | half[self.level] for s in have]
                for have, half in zip(self.slots, self.bits)
            ]
            self.level -= 1
            self.swaps(self.kept)
            if self.level == 0:
                self.early = [swap(v, "dp", self.size, 1) for v in self.kept]
        elif self.level == 0:
            self.others = self.pending
            self.level = -1
            self.pending = [swap(v, "dp", self.size, 1) for v in self.others]
        else:
            self.finished = True

    def complete(self, level):
        while not self.spreading or self.level > level:
            arrived([self])
            self.advance()

    def spread_first(self, *layout):
        self.complete(0)
        self.layout = layout
        slots = [s | core for have in self.slots for core in (0, 1) for s in have]
        arrays = [v for pair in zip(self.kept, self.early) for v in pair]
        self.outs = spread(self.index, self.size, arrays, slots, layout, None)

    def spread_second(self):
        self.complete(-1)
        slots = [
            s | bits[0] | core
            for have, bits in zip(self.slots, self.bits)
            for core in (0, 1)
            for s in have
        ]
        arrays = [v for pair in zip(self.others, self.pending) for v in pair]
        return spread(self.index, self.size, arrays, slots, self.layout, self.outs)


def arrived(sums, *values):
    count = [len(s.pending) for s in sums]
    out = list(tie(*[p for s in sums for p in s.pending], *values))
    for s, n in zip(sums, count):
        s.pending, out = out[:n], out[n:]
    return out


def computed(sums, *values):
    count = [len(s.kept) for s in sums]
    out = list(tie(*[p for s in sums for p in s.kept], *values))
    for s, n in zip(sums, count):
        s.kept, out = out[:n], out[n:]
    return out


def spread_kernel(quarter, layout, table_ref, *refs):
    ins, outs = refs[:4], refs[-len(layout) :]
    step = pl.program_id(0)
    for j, piece in enumerate(ins):

        @pl.when(step // quarter == j)
        def _(piece=piece):
            at = 0
            for out, (parts, columns, transposed) in zip(outs, layout):
                for c in range(parts):
                    block = piece[:, at : at + columns].astype(f32)
                    at += columns
                    if parts > 1:
                        out[c] = block
                    else:
                        out[...] = jnp.transpose(block) if transposed else block


def spread(index, size, arrays, slots, layout, into):
    table = index ^ jnp.array(slots, jnp.int32)
    quarter, half = size // 4, size // 2
    rows, width = arrays[0].shape[0] // quarter, arrays[0].shape[1]
    in_specs = [
        pl.BlockSpec(
            (rows, width),
            lambda i, t, at=j * quarter: (jnp.clip(i - at, 0, quarter - 1), 0),
        )
        for j in range(4)
    ]
    out_shape, out_specs = [], []
    for parts, columns, transposed in layout:
        if parts > 1:
            out_shape.append((parts, rows * size, 2 * columns))
            out_specs.append(
                pl.BlockSpec((parts, rows, columns), lambda i, t: (0, t[i], i // half))
            )
        elif transposed:
            out_shape.append((2 * columns, rows * size))
            out_specs.append(pl.BlockSpec((columns, rows), lambda i, t: (i // half, t[i])))
        else:
            out_shape.append((rows * size, 2 * columns))
            out_specs.append(pl.BlockSpec((rows, columns), lambda i, t: (t[i], i // half)))
    aliases = {}
    if into is not None:
        aliases = {1 + len(arrays) + k: k for k in range(len(layout))}
        in_specs += [pl.BlockSpec(memory_space=pl.ANY)] * len(layout)
        arrays = arrays + list(into)
    return pl.pallas_call(
        functools.partial(spread_kernel, quarter, layout),
        input_output_aliases=aliases,
        name="spread",
        out_shape=[jax.ShapeDtypeStruct(shape, f32) for shape in out_shape],
        grid_spec=pltpu.PrefetchScalarGridSpec(
            num_scalar_prefetch=1, grid=(size,), in_specs=in_specs, out_specs=out_specs
        ),
        compiler_params=pltpu.CompilerParams(vmem_limit_bytes=48 * 2**20),
        cost_estimate=pl.CostEstimate(
            flops=0, bytes_accessed=rows * width * size * 6, transcendentals=0
        ),
    )(table, *arrays)


def local(
    dp_size,
    hidden_in,
    gain,
    bias,
    w_qkv,
    b_qkv,
    w_dense,
    b_dense,
    w_fc1,
    b_fc1,
    w_fc2,
    b_fc2,
    cotangent,
    seq_lengths,
    padding,
    block_perm,
):
    tok_local, dim_local = hidden_in.shape
    model_width = gain.shape[0]
    heads = w_qkv.shape[2] // HD
    split = dp_size // heads
    subs = tok_local // BLK
    nblk = block_perm.shape[0]
    data_index = lax.axis_index("dp")
    tensor_index = lax.axis_index("tensor")
    pos_all, valid_all = token_table(seq_lengths, padding, block_perm)
    my_pos = lax.dynamic_slice_in_dim(pos_all, data_index * tok_local, tok_local)
    my_valid = lax.dynamic_slice_in_dim(valid_all, data_index * tok_local, tok_local)
    cosine, sine = rotary_tables(my_pos)
    cosine_all, sine_all = rotary_tables(jnp.arange(nblk * BLK, dtype=jnp.int32))
    place = jnp.concatenate([block_perm, pos_all[::BLK] // BLK])
    seq = jnp.stack([jnp.cumsum(seq_lengths) - seq_lengths, seq_lengths])
    rank = (data_index // heads).reshape(1).astype(jnp.int32)

    def to_heads(stacked):
        stacked = jnp.concatenate([stacked] * split) if split > 1 else stacked
        return lax.all_to_all(stacked, "dp", 0, 0, tiled=True)

    def to_tokens(stacked):
        got = lax.all_to_all(stacked, "dp", 0, 0, tiled=True)
        if split > 1:
            got = got.reshape(split, heads, *got.shape[1:]).astype(f32)
            got = jnp.sum(got, axis=0).astype(bf16)
        return got

    full_in = lax.all_gather(hidden_in.astype(bf16), "tensor", axis=1, tiled=True)
    grad_proj = lax.all_gather(cotangent.astype(bf16), "tensor", axis=1, tiled=True)
    w_back = row_major(jnp.transpose(w_qkv, (1, 2, 0)))
    full_in, w_back, cosine, sine, cosine_all, sine_all, place, seq = tie(
        full_in, w_back, cosine, sine, cosine_all, sine_all, place, seq
    )
    full_in = full_in.astype(f32)
    row_mean = jnp.mean(full_in, axis=-1, keepdims=True)
    centered = full_in - row_mean
    inv_std = lax.rsqrt(jnp.mean(centered * centered, axis=-1, keepdims=True) + epsilon)
    normal_x = centered * inv_std
    normed = (normal_x * gain + bias).astype(bf16)
    projections = (
        jnp.einsum("td,dcf->cft", normed, w_qkv, preferred_element_type=f32) + b_qkv[:, :, None]
    ).reshape(3, heads, HD, tok_local)
    turned = projections[:2, :, :ROT].reshape(2, heads, 2, HALF, tok_local)
    lower, upper = turned[:, :, 0], turned[:, :, 1]
    rotated = jnp.concatenate(
        [
            lower * cosine - upper * sine,
            upper * cosine + lower * sine,
            projections[:2, :, ROT:],
        ],
        axis=2,
    )
    packed = jnp.concatenate([rotated[0], rotated[1], projections[2]], axis=1).astype(bf16)
    packed, normed_late = tie(packed, normed)
    parts = to_heads(packed)
    hidden_pre = jnp.dot(normed, w_fc1, preferred_element_type=f32) + b_fc1
    activated = gelu_tanh(hidden_pre).astype(bf16)
    activated_t, normed_t = row_major(jnp.transpose(activated)), row_major(jnp.transpose(normed_late))
    value_fc2 = jnp.dot(activated, w_fc2, preferred_element_type=f32)
    parts, hidden_pre, activated_t, normed_t, value_fc2, grad_proj = tie(
        parts, hidden_pre, activated_t, normed_t, value_fc2, grad_proj
    )

    def new_sum(*pairs):
        made = PieceSum(data_index, dp_size, *pairs)
        made.across_cores()
        return made

    sum_fc2 = new_sum((activated_t, grad_proj, 1, 0))
    (grad_proj,) = computed([sum_fc2], grad_proj)
    grad_attended = jnp.einsum(
        "ed,td->et", w_dense, grad_proj, preferred_element_type=f32
    ).astype(bf16)
    (grad_attended,) = arrived([sum_fc2], grad_attended)
    grad_stack = to_heads(grad_attended.reshape(heads, HD, tok_local))
    sum_fc2.products()
    grad_proj, hidden_pre = computed([sum_fc2], grad_proj, hidden_pre)
    grad_act = jnp.einsum("td,fd->tf", grad_proj, w_fc2, preferred_element_type=f32)
    unused_value, gelu_back = jax.vjp(gelu_tanh, hidden_pre)
    grad_hidden = gelu_back(grad_act)[0].astype(bf16)
    (grad_hidden,) = arrived([sum_fc2], grad_hidden)
    sum_fc1 = new_sum((normed_t, grad_hidden, 1, 0))
    sum_fc1.kept = arrived([sum_fc1], *sum_fc1.kept)
    sum_fc2.advance()
    sum_fc1.pending = computed([sum_fc2], *sum_fc1.pending)
    sum_fc1.products()
    sum_fc1.kept = arrived([sum_fc2], *sum_fc1.kept)
    sum_fc2.advance()

    (parts,) = computed([sum_fc2, sum_fc1], parts)
    out_stack, lse, seq_out = attention_forward(place, seq, rank, parts, split)
    out_stack, grad_stack, lse = arrived([sum_fc2, sum_fc1], out_stack, grad_stack, lse)
    attended = to_tokens(out_stack).reshape(heads * HD, tok_local)
    sum_fc2.advance()
    sum_fc1.advance()
    (lse,) = computed([sum_fc2, sum_fc1], lse)
    grad_pieces = attention_backward(
        place, seq, rank, parts, grad_stack, lse, seq_out, cosine_all, sine_all, split
    )
    grad_pieces, attended, grad_hidden = arrived(
        [sum_fc2, sum_fc1], grad_pieces, attended, grad_hidden
    )

    grad_qkv = to_tokens(grad_pieces).reshape(heads, 3, HD, tok_local)
    grad_normed = jnp.einsum("tf,df->td", grad_hidden, w_fc1, preferred_element_type=f32)
    grad_normed, attended, *waiting = tie(
        grad_normed, attended, *sum_fc2.pending, *sum_fc1.pending
    )
    sum_fc2.pending = waiting[: len(sum_fc2.pending)]
    sum_fc1.pending = waiting[len(sum_fc2.pending) :]
    sum_fc1.advance()
    sum_fc2.advance()
    attended, *sum_fc1.kept = tie(attended, *sum_fc1.kept)
    partial_value = jnp.einsum(
        "et,ed->td", attended, w_dense, preferred_element_type=f32
    ) + value_fc2
    partial_value = partial_value.astype(bf16)
    projected = lax.psum_scatter(
        partial_value, "tensor", scatter_dimension=1, tiled=True
    ).astype(f32)
    grad_normed, partial_value = arrived([sum_fc1], grad_normed, partial_value)
    sum_fc1.advance()
    grad_qkv, grad_normed, *sum_fc1.kept = tie(grad_qkv, grad_normed, *sum_fc1.kept)
    branch = projected + b_dense + b_fc2
    output = hidden_in + branch
    valid_rows = my_valid.astype(f32)[:, None]
    sum_output = jnp.sum(output * output * valid_rows)
    sum_branch = jnp.sum(branch * branch * valid_rows)
    valid_count = jnp.sum(valid_all.astype(f32)) * model_width

    grad_b_fc1 = jnp.sum(grad_hidden.astype(f32), axis=0)
    grad_b_qkv = jnp.transpose(jnp.sum(grad_qkv.astype(f32), axis=3), (1, 0, 2))
    by_half = jnp.transpose(
        grad_qkv.reshape(2, heads // 2, 3, HD, tok_local), (0, 2, 1, 3, 4)
    ).reshape(3 * heads * HD, tok_local)
    sum_qkv = new_sum((normed_t, by_half, 1, 1), (grad_proj, attended, 0, 1))
    (grad_qkv,) = computed([sum_qkv], grad_qkv)
    grad_normed = row_major(
        grad_normed
        + jnp.einsum(
            "hcet,ched->td",
            grad_qkv,
            w_back.reshape(3, heads, HD, model_width),
            preferred_element_type=f32,
        )
    )
    grad_narrow = grad_normed.astype(bf16)
    (grad_narrow,) = arrived([sum_qkv, sum_fc1], grad_narrow)
    grad_local = lax.psum_scatter(
        grad_narrow, "tensor", scatter_dimension=1, tiled=True
    ).astype(f32)
    sum_qkv.products()
    sum_fc1.advance()
    sum_fc2.kept = computed([sum_qkv], *sum_fc2.kept)
    sum_fc2.spread_first((1, model_width // 2, False))
    sum_output, sum_branch, *sum_fc2.outs = arrived(
        [sum_qkv], sum_output, sum_branch, *sum_fc2.outs
    )
    sum_qkv.advance()
    sum_fc2.pending = computed([sum_qkv], *sum_fc2.pending)
    (grad_w_fc2,) = sum_fc2.spread_second()
    (grad_w_fc2,) = arrived([sum_qkv], grad_w_fc2)
    sum_qkv.advance()
    scaled = grad_normed * gain
    mean_sums = jnp.stack([jnp.sum(scaled, axis=1), jnp.sum(scaled * normal_x, axis=1)])
    shared = jnp.concatenate([mean_sums.reshape(-1), sum_output[None], sum_branch[None]])
    sum_fc1.complete(0)
    sum_fc1.early = computed([sum_qkv], *sum_fc1.early)
    sum_fc1.spread_first((1, w_fc1.shape[1] // 2, False))
    sum_fc1.outs = arrived([sum_qkv], *sum_fc1.outs)
    sum_qkv.advance()
    sum_fc1.pending = computed([sum_qkv], *sum_fc1.pending)
    (grad_w_fc1,) = sum_fc1.spread_second()
    shared = all_sum(shared, "tensor", model_width // dim_local)
    mean_sums = shared[:-2].reshape(2, tok_local) / model_width
    mean_one, mean_two = mean_sums[0][:, None], mean_sums[1][:, None]
    gain_local = lax.dynamic_slice_in_dim(gain, tensor_index * dim_local, dim_local)
    normal_local = lax.dynamic_slice_in_dim(normal_x, tensor_index * dim_local, dim_local, 1)
    grad_input = cotangent + inv_std * (
        grad_local * gain_local - mean_one - normal_local * mean_two
    )
    late = jnp.concatenate(
        [
            jnp.sum(grad_local * normal_local, axis=0),
            jnp.sum(grad_local, axis=0),
            jnp.sum(cotangent, axis=0),
            grad_b_fc1,
            grad_b_qkv.reshape(-1),
            shared[-2:],
        ]
    )
    cuts = [dim_local, 2 * dim_local, 3 * dim_local, 3 * dim_local + grad_b_fc1.shape[0]]
    late = all_sum(late, "dp", dp_size)
    sum_qkv.complete(0)
    sum_qkv.early[0], grad_w_fc1 = tie(sum_qkv.early[0], grad_w_fc1)
    sum_qkv.spread_first((3, heads * HD // 2, False), (1, heads * HD // 2, True))
    sum_qkv.outs = arrived([sum_qkv], *sum_qkv.outs)
    sum_qkv.advance()
    sum_qkv.complete(-1)
    grad_w_qkv, grad_w_dense = sum_qkv.spread_second()
    late, grad_w_dense = tie(late, grad_w_dense)
    grad_w_qkv = jnp.transpose(grad_w_qkv, (1, 0, 2))
    totals = late[-2:]
    rms = jnp.sqrt(totals / valid_count)
    bias_grad = late[cuts[1] : cuts[2]]
    return (
        output,
        grad_input,
        late[: cuts[0]],
        late[cuts[0] : cuts[1]],
        grad_w_qkv,
        late[cuts[3] : -2].reshape(3, heads * HD),
        grad_w_dense,
        bias_grad,
        grad_w_fc1,
        late[cuts[2] : cuts[3]],
        grad_w_fc2,
        bias_grad,
        rms[0],
        rms[1],
    )


def solution(mesh):
    return jax.shard_map(
        functools.partial(local, mesh.shape["dp"]),
        mesh=mesh,
        in_specs=(
            P("dp", "tensor"),
            P(),
            P(),
            P(None, None, "tensor"),
            P(None, "tensor"),
            P("tensor", None),
            P("tensor"),
            P(None, "tensor"),
            P("tensor"),
            P("tensor", None),
            P("tensor"),
            P("dp", "tensor"),
            P(),
            P(),
            P(),
        ),
        out_specs=(
            P("dp", "tensor"),
            P("dp", "tensor"),
            P("tensor"),
            P("tensor"),
            P(None, None, "tensor"),
            P(None, "tensor"),
            P("tensor", None),
            P("tensor"),
            P(None, "tensor"),
            P("tensor"),
            P("tensor", None),
            P("tensor"),
            P(),
            P(),
        ),
        check_vma=False,
    )
```
